1024 devices in a mesh: ctx: 16 (over z, core), head: 8 (over x), band: 8 (over y).
Axes of the slice: x: 8, y: 8, z: 8, core: 2. Of those that a mesh axis runs over, the one named last changes fastest.
Arguments:
- queries: bfloat16 [131072, 1024], P(('band', 'ctx', 'head')), parts along dimension 0, may hold values from -6 to 6
- key_states: bfloat16 [131072, 1024], P(('band', 'ctx', 'head')), parts along dimension 0, may hold values from -6 to 6
- value_states: bfloat16 [131072, 1024], P(('band', 'ctx', 'head')), parts along dimension 0, may hold values from -6 to 6
- grad_output: bfloat16 [131072, 1024], P(('band', 'ctx', 'head')), parts along dimension 0, may hold values from -24 to 24
- block_slot: int32 [2048], P('band'), parts along dimension 0, may hold values from 0 to 255, as said below
- neighbours: int32 [2048, 8], P('band'), parts along dimension 0, may hold values from 0 to 255, as said below
Outputs:
- grad_queries: bfloat16 [131072, 1024], P(('band', 'ctx', 'head')), parts along dimension 0
- grad_keys: bfloat16 [131072, 1024], P(('band', 'ctx', 'head')), parts along dimension 0
- grad_values: bfloat16 [131072, 1024], P(('band', 'ctx', 'head')), parts along dimension 0
The draws below stay inside these ranges and needn't reach their ends.
There are 8 independent parts, one for each index of `band`. The reference program is written for one: setup_inputs(seed, part) draws one part's arguments, and reference() takes and returns one part's arrays. A program takes and returns all parts, laid end to end along the dimension named above; each array names one. Nothing has to cross between parts.
Inputs may be any that keep to these rules, and one draw needn't show every extreme that they name: `block_slot`: a permutation of the 256 slots. `neighbours`: entry 0 of row b is b. The slot of every other entry lies on a ctx index, slot // 16, at most 1 away cyclically from that of b. These entries are distinct where at least 7 such blocks exist, and else repeat.
All inputs are finite; a program needn't handle non-finite values.
Results may differ from the reference program's by a relative error of at most 0.0088.
Values may be sent and summed in bfloat16 or wider, within the bound.
A program may use at most 128 MiB of HBM per device.

```python
import jax
import jax.numpy as jnp
from jax import lax

HEADS = 16
HEAD_DIM = 64
D = 1024
BLOCK_TOK = 64
NBR = 8
REACH = 1
BLK_DEV = 16
BLOCKS = 256
TOKENS = 16384


def layout_draw(key):
    per_device = BLK_DEV
    dev_count = BLOCKS // BLK_DEV
    rotation = jax.random.randint(jax.random.fold_in(key, 11), (), 0, dev_count)
    inner_scores = jax.random.randint(jax.random.fold_in(key, 12), (dev_count, per_device), 0, 1 << 20)
    inner_order = jnp.argsort(inner_scores * per_device + jnp.arange(per_device)[None, :], axis=1)
    sphere = jnp.arange(BLOCKS, dtype=jnp.int32)
    home_dev = (sphere // per_device + rotation) % dev_count
    slot_of = (home_dev * per_device + inner_order[sphere // per_device, sphere % per_device]).astype(jnp.int32)
    sphere_of = jnp.zeros((BLOCKS,), jnp.int32).at[slot_of].set(sphere)
    deltas = sorted(set((offset % dev_count for offset in range(-REACH, REACH + 1))))
    delta_table = jnp.array(deltas, dtype=jnp.int32)
    cand_count = len(deltas) * per_device
    candidates = (home_dev[:, None, None] + delta_table[None, :, None]) % dev_count * per_device
    candidates = (candidates + jnp.arange(per_device, dtype=jnp.int32)[None, None, :]).reshape(BLOCKS, cand_count)
    draw_scores = jax.random.randint(jax.random.fold_in(key, 13), (BLOCKS, cand_count), 0, 1 << 20)
    draw_scores = draw_scores * cand_count + jnp.arange(cand_count)[None, :]
    draw_scores = jnp.where(candidates == slot_of[:, None], -1, draw_scores)
    ranking = jnp.argsort(-draw_scores, axis=1)[:, :cand_count - 1]
    picked = ranking[:, jnp.arange(NBR - 1) % (cand_count - 1)]
    chosen_slots = jnp.take_along_axis(candidates, picked, axis=1)
    neighbour_rows = jnp.concatenate([sphere[:, None], sphere_of[chosen_slots]], axis=1)
    return (slot_of, neighbour_rows.astype(jnp.int32))


def draw_block_slot(key, part):
    return layout_draw(key)[0]


def draw_neighbours(key, part):
    return layout_draw(key)[1]


def draw_queries(key, part):
    return jnp.clip(jax.random.normal(jax.random.fold_in(key, 23), (TOKENS, D), jnp.float32), -6.0, 6.0).astype(jnp.bfloat16)


def draw_key_states(key, part):
    return jnp.clip(jax.random.normal(jax.random.fold_in(key, 24), (TOKENS, D), jnp.float32), -6.0, 6.0).astype(jnp.bfloat16)


def block_levels(key, shape, cuts, least, top_value):
    factor_of = 1.0
    for position, parts in cuts:
        steps = jax.random.uniform(jax.random.fold_in(jax.random.fold_in(key, 6), position), (parts,), jnp.float32, least / len(cuts), top_value / len(cuts))
        factor_of = factor_of * jnp.repeat(jnp.exp(steps), shape[position] // parts).reshape((-1,) + (1,) * (len(shape) - 1 - position))
    return factor_of


def centred(key, extent, scale, reach, pieces=(), kind=jnp.bfloat16):
    entries = jax.random.normal(key, extent, jnp.float32) * scale
    if len(pieces) > 0:
        entries = block_levels(key, extent, pieces, -0.22, 0.18) * entries
    return jnp.clip(entries, min=-reach, max=reach).astype(kind)


def setup_inputs(seed: int = 0, part: int = 0) -> dict:
    splits = jax.random.split(jax.random.key(seed), 7)
    part_keys = jax.random.split(jax.random.fold_in(splits[6], part), 7)
    queries = draw_queries(jax.random.fold_in(jax.random.fold_in(splits[6], part), 71), part)
    key_states = draw_key_states(jax.random.fold_in(jax.random.fold_in(splits[6], part), 71), part)
    value_states = centred(part_keys[2], (TOKENS, D), 1.0, 6.0, ((0, 128),))
    grad_output = jnp.clip(jax.random.uniform(part_keys[3], (TOKENS, D), jnp.float32, -24.0, 24.0) * block_levels(part_keys[3], (TOKENS, D), ((0, 128),), -0.4, 0.0), -24.0, 24.0).astype(jnp.bfloat16)
    block_slot = draw_block_slot(jax.random.fold_in(jax.random.fold_in(splits[6], part), 71), part)
    neighbours = draw_neighbours(jax.random.fold_in(jax.random.fold_in(splits[6], part), 71), part)
    return dict(queries=queries, key_states=key_states, value_states=value_states, grad_output=grad_output, block_slot=block_slot, neighbours=neighbours)


def reference(queries, key_states, value_states, grad_output, block_slot, neighbours):
    softmax_scale = HEAD_DIM ** -0.5
    slot_ids = jnp.arange(BLOCKS, dtype=jnp.int32)
    sphere_of = jnp.zeros((BLOCKS,), jnp.int32).at[block_slot].set(slot_ids)
    listed = block_slot[neighbours[sphere_of]].astype(jnp.int32)
    block_shape = (BLOCKS, BLOCK_TOK, HEADS, HEAD_DIM)
    query_blocks = queries.reshape(block_shape)
    key_blocks = key_states.reshape(block_shape)
    value_blocks = value_states.reshape(block_shape)
    grad_blocks = grad_output.reshape(block_shape)

    def one_slot(carried, slot_now):
        grad_key_acc, grad_val_acc = carried
        chosen = listed[slot_now]
        query_now = query_blocks[slot_now].astype(jnp.float32)
        grad_now = grad_blocks[slot_now].astype(jnp.float32)
        key_now = key_blocks[chosen].reshape(NBR * BLOCK_TOK, HEADS, HEAD_DIM).astype(jnp.float32)
        value_now = value_blocks[chosen].reshape(NBR * BLOCK_TOK, HEADS, HEAD_DIM).astype(jnp.float32)
        scores = jnp.einsum("qhd,khd->hqk", query_now, key_now) * softmax_scale
        probability = jax.nn.softmax(scores, axis=-1)
        grad_prob = jnp.einsum("qhd,khd->hqk", grad_now, value_now)
        row_delta = jnp.sum(probability * grad_prob, axis=-1, keepdims=True)
        grad_score = probability * (grad_prob - row_delta)
        prob_low = lax.optimization_barrier(probability.astype(jnp.bfloat16)).astype(jnp.float32)
        score_low = lax.optimization_barrier(grad_score.astype(jnp.bfloat16)).astype(jnp.float32)
        value_part = jnp.einsum("hqk,qhd->khd", prob_low, grad_now)
        key_part = jnp.einsum("hqk,qhd->khd", score_low, query_now) * softmax_scale
        query_grad = (jnp.einsum("hqk,khd->qhd", score_low, key_now) * softmax_scale).astype(jnp.bfloat16)
        grad_key_acc = grad_key_acc.at[chosen].add(key_part.reshape(NBR, BLOCK_TOK, HEADS, HEAD_DIM))
        grad_val_acc = grad_val_acc.at[chosen].add(value_part.reshape(NBR, BLOCK_TOK, HEADS, HEAD_DIM))
        return (grad_key_acc, grad_val_acc), query_grad

    start = (jnp.zeros(block_shape, jnp.float32), jnp.zeros(block_shape, jnp.float32))
    (grad_key_acc, grad_val_acc), query_grads = lax.scan(one_slot, start, slot_ids)
    grad_queries = query_grads.reshape(TOKENS, D)
    grad_keys = grad_key_acc.reshape(TOKENS, D).astype(jnp.bfloat16)
    grad_values = grad_val_acc.reshape(TOKENS, D).astype(jnp.bfloat16)
    return (grad_queries, grad_keys, grad_values)
```

```python
import functools
import math

import jax
import jax.numpy as jnp
from jax import lax
from jax.experimental import pallas as pl
from jax.experimental.pallas import tpu as pltpu
from jax.sharding import PartitionSpec as P

HEAD_DIM = 64
BLOCK_TOK = 64
NBR = 8
MESH = pl.DeviceIdType.MESH
NT = (((1,), (1,)), ((), ()))
NN = (((1,), (0,)), ((), ()))
TN = (((0,), (0,)), ((), ()))


def at_step(step, H):
    return lax.rem(jnp.where(step % 2 == 1, (step + 1) // 2, H - step // 2), H)


def table_kernel(per_ctx, ctx_size, heads, slot_ref, nbr_ref, out_ref, inverse):
    ctx = lax.axis_index("ctx")
    h = lax.axis_index("head")
    per_chunk = per_ctx // heads
    slots = slot_ref.shape[0]
    pairs = per_ctx * NBR
    base = ctx * per_ctx

    def invert(step, carry):
        for k in range(8):
            b = step * 8 + k
            inverse[slot_ref[b]] = b
        return carry

    lax.fori_loop(0, slots // 8, invert, 0)

    def clear(t, carry):
        out_ref[2 * pairs + t] = pairs
        return carry

    lax.fori_loop(0, 3 * per_ctx, clear, 0)

    def one(turn, carry):
        chunk = lax.rem(h + heads - at_step(turn // per_chunk, heads), heads)
        s = chunk * per_chunk + turn % per_chunk
        sphere = inverse[base + s]
        for n in range(NBR):
            slot = slot_ref[nbr_ref[n, sphere]]
            gap = slot // per_ctx - ctx + 1
            gap = jnp.where(gap < 0, gap + ctx_size, gap)
            gap = jnp.where(gap >= ctx_size, gap - ctx_size, gap)
            target = gap * per_ctx + slot % per_ctx
            pair = s * NBR + n
            out_ref[pair] = target
            out_ref[pairs + pair] = out_ref[2 * pairs + target]
            out_ref[2 * pairs + target] = pair
        return carry

    lax.fori_loop(0, per_ctx, one, 0)


def main_kernel(heads, ctx_size, table, q_in, k_in, v_in, g_in, dq_out, dk_out, dv_out,
                q_loc, g_loc, k_span, v_span, run_k, run_v, dq_stage, part_k, part_v, back_k, back_v, sum_k, sum_v,
                in_send, in_recv, fwd_send, fwd_recv, dq_send, dq_recv, ret_send, ret_recv, out_send, out_recv):
    H = heads
    h = lax.axis_index("head")
    c = lax.axis_index("ctx")
    per_chunk = q_in.shape[0]
    T = H * per_chunk
    per_ctx = T
    pairs = per_ctx * NBR
    scale = HEAD_DIM ** -0.5
    ctx_prev = lax.rem(c + ctx_size - 1, ctx_size)
    ctx_next = lax.rem(c + 1, ctx_size)
    ctx_peer = (ctx_prev, ctx_next)

    def peer(d):
        return lax.rem(h + d, H)

    def source(d):
        return lax.rem(h + H - d, H)

    def rows(base, chunk):
        return pl.ds(base + chunk * per_chunk, per_chunk)

    def cols(chunk):
        return pl.ds(pl.multiple_of(chunk * 128, 128), 128)

    barrier = pltpu.get_barrier_semaphore()
    for d in range(1, H):
        pl.semaphore_signal(barrier, inc=1, device_id={"head": peer(d)}, device_id_type=MESH)
    for p in ctx_peer:
        pl.semaphore_signal(barrier, inc=1, device_id={"ctx": p}, device_id_type=MESH)
    pl.semaphore_wait(barrier, H + 1)

    order = [0]
    for step in range(1, H):
        order.append(((step + 1) // 2 if step % 2 else H - step // 2) % H)

    incoming = ((k_in, k_span, T), (v_in, v_span, T), (q_in, q_loc, 0), (g_in, g_loc, 0))

    def in_copy(t, d):
        src, dst, base = incoming[t]
        return pltpu.make_async_remote_copy(
            src_ref=src.at[:, :, cols(peer(d))], dst_ref=dst.at[rows(base, h)],
            send_sem=in_send.at[t, d], recv_sem=in_recv.at[t, d],
            device_id={"head": peer(d)}, device_id_type=MESH)

    def in_own(t):
        src, dst, base = incoming[t]
        return pltpu.make_async_copy(src.at[:, :, cols(h)], dst.at[rows(base, h)], in_recv.at[t, 0])

    def in_wait(t, d):
        src, dst, base = incoming[t]
        pltpu.make_async_remote_copy(
            src_ref=src.at[:, :, cols(peer(d))], dst_ref=dst.at[rows(base, source(d))],
            send_sem=in_send.at[t, d], recv_sem=in_recv.at[t, d],
            device_id={"head": peer(d)}, device_id_type=MESH).wait_recv()

    for t in range(4):
        in_own(t).start()
        for d in order[1:]:
            in_copy(t, d).start()

    def fwd_copy(t, d, way):
        span = incoming[t][1]
        chunk = source(d)
        return pltpu.make_async_remote_copy(
            src_ref=span.at[rows(T, chunk)],
            dst_ref=span.at[rows(2 * T if way == 0 else 0, chunk)],
            send_sem=fwd_send.at[t, d, way], recv_sem=fwd_recv.at[t, d, way],
            device_id={"ctx": ctx_peer[way]}, device_id_type=MESH)

    run_k[pairs] = jnp.zeros(run_k.shape[1:], jnp.float32)
    run_v[pairs] = jnp.zeros(run_v.shape[1:], jnp.float32)

    for t in range(2):
        for d in order:
            if d == 0:
                in_own(t).wait()
            else:
                in_wait(t, d)
            for way in range(2):
                fwd_copy(t, d, way).start()

    def fwd_wait(t, d, way):
        span = incoming[t][1]
        chunk = source(d)
        pltpu.make_async_remote_copy(
            src_ref=span.at[rows(T, chunk)],
            dst_ref=span.at[rows(2 * T if way == 0 else 0, chunk)],
            send_sem=fwd_send.at[t, d, way], recv_sem=fwd_recv.at[t, d, way],
            device_id={"ctx": ctx_peer[way]}, device_id_type=MESH).wait_recv()

    for t in range(2):
        for d in order:
            for way in range(2):
                fwd_wait(t, d, way)

    low = (lax.broadcasted_iota(jnp.int32, (1, 128), 1) < HEAD_DIM).astype(jnp.float32)
    low_mask = low.astype(jnp.bfloat16)
    high_mask = (1.0 - low).astype(jnp.bfloat16)
    low_lanes = lax.broadcasted_iota(jnp.int32, (BLOCK_TOK, 128), 1) < HEAD_DIM
    exp_scale = scale * math.log2(math.e)

    def one_block(s):
        q = q_loc[s]
        g = g_loc[s]
        wq = jnp.concatenate([q * low_mask, q * high_mask], axis=0)
        wg = jnp.concatenate([g * low_mask, g * high_mask], axis=0)
        places = [table[s * NBR + n] for n in range(NBR)]
        ks = jnp.concatenate([k_span[p] for p in places], axis=0)
        vs = jnp.concatenate([v_span[p] for p in places], axis=0)
        scores = lax.dot_general(ks, wq, NT, preferred_element_type=jnp.float32)
        top = jnp.max(scores, axis=0, keepdims=True)
        weights = jnp.exp2((scores - top) * exp_scale)
        inverse = 1.0 / jnp.sum(weights, axis=0, keepdims=True)
        prob = weights * inverse
        grad_prob = lax.dot_general(vs, wg, NT, preferred_element_type=jnp.float32)
        delta = jnp.sum(prob * grad_prob, axis=0, keepdims=True)
        score_low = (prob * (grad_prob - delta)).astype(jnp.bfloat16)
        prob_low = prob.astype(jnp.bfloat16)
        dv = lax.dot_general(prob_low, wg, NN, preferred_element_type=jnp.float32)
        dk = lax.dot_general(score_low, wq, NN, preferred_element_type=jnp.float32)
        dq = lax.dot_general(score_low, ks, TN, preferred_element_type=jnp.float32)
        dq = jnp.where(low_lanes, dq[:BLOCK_TOK], dq[BLOCK_TOK:]) * scale
        dq_stage[s] = dq.astype(jnp.bfloat16)
        for n in range(NBR):
            pair = s * NBR + n
            before = table[pairs + pair]
            part = slice(n * BLOCK_TOK, (n + 1) * BLOCK_TOK)
            run_k[pair] = dk[part] + run_k[before]
            run_v[pair] = dv[part] + run_v[before]

    def dq_copy(d):
        chunk = source(d)
        return pltpu.make_async_remote_copy(
            src_ref=dq_stage.at[rows(0, chunk)], dst_ref=dq_out.at[:, :, cols(h)],
            send_sem=dq_send.at[d], recv_sem=dq_recv.at[d],
            device_id={"head": chunk}, device_id_type=MESH)

    def dq_own():
        return pltpu.make_async_copy(dq_stage.at[rows(0, h)], dq_out.at[:, :, cols(h)], dq_recv.at[0])

    def one_step(step, carry):
        d = at_step(step, H)
        chunk = source(d)

        @pl.when(step == 0)
        def _():
            in_own(2).wait()
            in_own(3).wait()

        @pl.when(step > 0)
        def _():
            in_wait(2, d)
            in_wait(3, d)

        for k in range(per_chunk):
            one_block(chunk * per_chunk + k)

        @pl.when(step == 1)
        def _():
            dq_own().start()

        @pl.when(step > 1)
        def _():
            dq_copy(at_step(step - 1, H)).start()

        return carry

    lax.fori_loop(0, H, one_step, 0)
    dq_copy(order[H - 1]).start()

    last = 2 * pairs
    back_order = order[::-1]

    def ret_copy(d, way, which):
        chunk = peer(d)
        part = (part_k, part_v)[which]
        back = (back_k, back_v)[which]
        return pltpu.make_async_remote_copy(
            src_ref=part.at[rows(way * T, chunk)], dst_ref=back.at[rows(way * T, chunk)],
            send_sem=ret_send.at[which, d, way], recv_sem=ret_recv.at[which, d, way],
            device_id={"ctx": ctx_peer[way]}, device_id_type=MESH)

    for d in back_order:
        chunk = peer(d)
        for way in range(2):
            region = 0 if way == 0 else 2
            for k in range(per_chunk):
                block = chunk * per_chunk + k
                end = table[last + region * per_ctx + block]
                part_k[way * T + block] = (run_k[end] * scale).astype(jnp.bfloat16)
                part_v[way * T + block] = run_v[end].astype(jnp.bfloat16)
        for way in range(2):
            for which in range(2):
                ret_copy(d, way, which).start()

    def out_copy(d, which):
        chunk = peer(d)
        return pltpu.make_async_remote_copy(
            src_ref=(sum_k, sum_v)[which].at[rows(0, chunk)], dst_ref=(dk_out, dv_out)[which].at[:, :, cols(h)],
            send_sem=out_send.at[which, d], recv_sem=out_recv.at[which, d],
            device_id={"head": chunk}, device_id_type=MESH)

    def out_own(which):
        return pltpu.make_async_copy(
            (sum_k, sum_v)[which].at[rows(0, h)], (dk_out, dv_out)[which].at[:, :, cols(h)], out_recv.at[which, 0])

    for d in back_order:
        chunk = peer(d)
        for way in range(2):
            for which in range(2):
                ret_copy(d, way, which).wait_recv()
        for k in range(per_chunk):
            block = chunk * per_chunk + k
            end = table[last + per_ctx + block]
            sum_k[block] = (run_k[end] * scale + back_k[block].astype(jnp.float32)
                            + back_k[T + block].astype(jnp.float32)).astype(jnp.bfloat16)
            sum_v[block] = (run_v[end] + back_v[block].astype(jnp.float32)
                            + back_v[T + block].astype(jnp.float32)).astype(jnp.bfloat16)
        for which in range(2):
            if d == 0:
                out_own(which).start()
            else:
                out_copy(d, which).start()

    dq_own().wait()
    for which in range(2):
        out_own(which).wait()
    for d in order[1:]:
        for t in range(4):
            in_copy(t, d).wait_send()
        dq_copy(d).wait_send()
        pltpu.make_async_remote_copy(
            src_ref=dq_stage.at[rows(0, peer(d))], dst_ref=dq_out.at[:, :, cols(peer(d))],
            send_sem=dq_send.at[d], recv_sem=dq_recv.at[d],
            device_id={"head": peer(d)}, device_id_type=MESH).wait_recv()
        for which in range(2):
            out_copy(d, which).wait_send()
            pltpu.make_async_remote_copy(
                src_ref=(sum_k, sum_v)[which].at[rows(0, source(d))],
                dst_ref=(dk_out, dv_out)[which].at[:, :, cols(source(d))],
                send_sem=out_send.at[which, d], recv_sem=out_recv.at[which, d],
                device_id={"head": source(d)}, device_id_type=MESH).wait_recv()
    for d in order:
        for way in range(2):
            for which in range(2):
                fwd_copy(which, d, way).wait_send()
                ret_copy(d, way, which).wait_send()


def body(queries, key_states, value_states, grad_output, block_slot, neighbours):
    H = lax.axis_size("head")
    C = lax.axis_size("ctx")
    rows, width = queries.shape
    chunk = rows // BLOCK_TOK
    per_ctx = chunk * H
    pairs = per_ctx * NBR
    entries = -(-(2 * pairs + 3 * per_ctx) // 128) * 128
    T = per_ctx
    smem = pl.BlockSpec(memory_space=pltpu.SMEM)
    hbm = pl.BlockSpec(memory_space=pl.ANY)
    table = pl.pallas_call(
        functools.partial(table_kernel, per_ctx, C, H),
        out_shape=jax.ShapeDtypeStruct((entries,), jnp.int32),
        in_specs=[smem, smem],
        out_specs=smem,
        scratch_shapes=[pltpu.SMEM((block_slot.shape[0],), jnp.int32)],
        name="tables",
    )(block_slot, neighbours.T)
    out = jax.ShapeDtypeStruct((chunk, BLOCK_TOK, width), jnp.bfloat16)
    dma = pltpu.SemaphoreType.DMA
    low = jnp.bfloat16
    grads = pl.pallas_call(
        functools.partial(main_kernel, H, C),
        out_shape=(out, out, out),
        in_specs=[smem] + [hbm] * 4,
        out_specs=(hbm, hbm, hbm),
        scratch_shapes=[
            pltpu.VMEM((T, BLOCK_TOK, 128), low), pltpu.VMEM((T, BLOCK_TOK, 128), low),
            pltpu.VMEM((3 * T, BLOCK_TOK, 128), low), pltpu.VMEM((3 * T, BLOCK_TOK, 128), low),
            pltpu.VMEM((pairs + 1, BLOCK_TOK, 128), jnp.float32),
            pltpu.VMEM((pairs + 1, BLOCK_TOK, 128), jnp.float32),
            pltpu.VMEM((T, BLOCK_TOK, 128), low),
            pltpu.VMEM((2 * T, BLOCK_TOK, 128), low), pltpu.VMEM((2 * T, BLOCK_TOK, 128), low),
            pltpu.VMEM((2 * T, BLOCK_TOK, 128), low), pltpu.VMEM((2 * T, BLOCK_TOK, 128), low),
            pltpu.VMEM((T, BLOCK_TOK, 128), low), pltpu.VMEM((T, BLOCK_TOK, 128), low),
            dma((4, H)), dma((4, H)), dma((2, H, 2)), dma((2, H, 2)), dma((H,)), dma((H,)),
            dma((2, H, 2)), dma((2, H, 2)), dma((2, H)), dma((2, H)),
        ],
        compiler_params=pltpu.CompilerParams(collective_id=0, has_side_effects=True, vmem_limit_bytes=56 * 2**20),
        name="attention",
    )(table, *(x.reshape(chunk, BLOCK_TOK, width) for x in (queries, key_states, value_states, grad_output)))
    return tuple(x.reshape(rows, width) for x in grads)


def solution(mesh):
    tokens = P(("band", "ctx", "head"), None)
    in_specs = (tokens, tokens, tokens, tokens, P("band"), P("band", None))
    return jax.shard_map(body, mesh=mesh, in_specs=in_specs, out_specs=(tokens, tokens, tokens), check_vma=False)
```

```python
import functools
import math

import jax
import jax.numpy as jnp
from jax import lax
from jax.experimental import pallas as pl
from jax.experimental.pallas import tpu as pltpu
from jax.sharding import PartitionSpec as P

HEAD_DIM = 64
BLOCK_TOK = 64
NBR = 8
MESH = pl.DeviceIdType.MESH
NT = (((1,), (1,)), ((), ()))
NN = (((1,), (0,)), ((), ()))
TN = (((0,), (0,)), ((), ()))


def at_step(step, H):
    return lax.rem(jnp.where(step % 2 == 1, (step + 1) // 2, H - step // 2), H)


def copy_kernel(*refs):
    half = len(refs) // 2
    copies = [pltpu.make_async_copy(refs[i], refs[half + i], refs[-1].at[i]) for i in range(half)]
    for copy in copies:
        copy.start()
    for copy in copies:
        copy.wait()


def main_kernel(heads, ctx_size, slot_in, nbr_in, q_in, k_in, v_in, g_in, dq_out, dk_out, dv_out,
                slot_ref, nbr_ref, table_vec, table, table_sem,
                q_loc, g_loc, k_span, v_span, run_k, run_v, dq_stage, part_k, part_v, back_k, back_v, sum_k, sum_v,
                in_send, in_recv, fwd_send, fwd_recv, dq_send, dq_recv, ret_send, ret_recv, out_send, out_recv):
    H = heads
    h = lax.axis_index("head")
    c = lax.axis_index("ctx")
    per_chunk = q_in.shape[0]
    T = H * per_chunk
    per_ctx = T
    pairs = per_ctx * NBR
    scale = HEAD_DIM ** -0.5
    ctx_prev = lax.rem(c + ctx_size - 1, ctx_size)
    ctx_next = lax.rem(c + 1, ctx_size)
    ctx_peer = (ctx_prev, ctx_next)

    def peer(d):
        return lax.rem(h + d, H)

    def source(d):
        return lax.rem(h + H - d, H)

    def rows(base, chunk):
        return pl.ds(base + chunk * per_chunk, per_chunk)

    def cols(chunk):
        return pl.ds(pl.multiple_of(chunk * 128, 128), 128)

    slot_copy = pltpu.make_async_copy(slot_in, slot_ref, table_sem.at[2])
    nbr_copy = pltpu.make_async_copy(nbr_in, nbr_ref, table_sem.at[3])
    slot_copy.start()
    nbr_copy.start()
    barrier = pltpu.get_barrier_semaphore()
    for d in range(1, H):
        pl.semaphore_signal(barrier, inc=1, device_id={"head": peer(d)}, device_id_type=MESH)
    for p in ctx_peer:
        pl.semaphore_signal(barrier, inc=1, device_id={"ctx": p}, device_id_type=MESH)
    pl.semaphore_wait(barrier, H + 1)

    order = [0]
    for step in range(1, H):
        order.append(((step + 1) // 2 if step % 2 else H - step // 2) % H)

    incoming = ((k_in, k_span, T), (v_in, v_span, T), (q_in, q_loc, 0), (g_in, g_loc, 0))

    def in_copy(t, d):
        src, dst, base = incoming[t]
        return pltpu.make_async_remote_copy(
            src_ref=src.at[:, :, cols(peer(d))], dst_ref=dst.at[rows(base, h)],
            send_sem=in_send.at[t, d], recv_sem=in_recv.at[t, d],
            device_id={"head": peer(d)}, device_id_type=MESH)

    def in_own(t):
        src, dst, base = incoming[t]
        return pltpu.make_async_copy(src.at[:, :, cols(h)], dst.at[rows(base, h)], in_recv.at[t, 0])

    def in_wait(t, d):
        src, dst, base = incoming[t]
        pltpu.make_async_remote_copy(
            src_ref=src.at[:, :, cols(peer(d))], dst_ref=dst.at[rows(base, source(d))],
            send_sem=in_send.at[t, d], recv_sem=in_recv.at[t, d],
            device_id={"head": peer(d)}, device_id_type=MESH).wait_recv()

    for t in range(4):
        in_own(t).start()
        for d in order[1:]:
            in_copy(t, d).start()

    def fwd_copy(t, d, way):
        span = incoming[t][1]
        chunk = source(d)
        return pltpu.make_async_remote_copy(
            src_ref=span.at[rows(T, chunk)],
            dst_ref=span.at[rows(2 * T if way == 0 else 0, chunk)],
            send_sem=fwd_send.at[t, d, way], recv_sem=fwd_recv.at[t, d, way],
            device_id={"ctx": ctx_peer[way]}, device_id_type=MESH)

    slot_copy.wait()
    nbr_copy.wait()
    slots = slot_ref.shape[1]
    slot_row = slot_ref[...]
    nbr = nbr_ref[...]
    slot_lane = lax.broadcasted_iota(jnp.int32, (NBR, slots), 1)
    lane = lax.broadcasted_iota(jnp.int32, (NBR, 128), 1)
    own = lane * NBR + lax.broadcasted_iota(jnp.int32, (NBR, 128), 0)
    targets = jnp.zeros((NBR, 128), jnp.int32)
    for turn in range(per_ctx):
        s = source(order[turn // per_chunk]) * per_chunk + turn % per_chunk
        near = jnp.sum(jnp.where(slot_row == c * per_ctx + s, nbr, 0), axis=1, keepdims=True)
        slot = jnp.sum(jnp.where(slot_lane == near, slot_row, 0), axis=1, keepdims=True)
        target = jnp.zeros_like(slot)
        for region, owner in enumerate((ctx_prev, c, ctx_next)):
            local = slot - owner * per_ctx
            target = jnp.where((local >= 0) & (local < per_ctx), local + region * per_ctx, target)
        targets = jnp.where(lane == turn, target, targets)
    table_vec[0] = targets
    first_half = pltpu.make_async_copy(table_vec.at[pl.ds(0, 1)], table.at[pl.ds(0, 1)], table_sem.at[0])
    first_half.start()
    first_half.wait()

    def chain(turn, carry):
        before, last = carry
        for n in range(NBR):
            target = table[0, n, turn]
            pair = turn * NBR + n
            before = jnp.where((targets == target) & (own > pair), pair, before)
            last = jnp.where(lane == target, pair, last)
        return before, last

    nothing = jnp.full((NBR, 128), pairs, jnp.int32)
    before, last = lax.fori_loop(0, per_ctx, chain, (nothing, nothing))
    table_vec[1] = before
    table_vec[2] = last
    second_half = pltpu.make_async_copy(table_vec.at[pl.ds(1, 2)], table.at[pl.ds(1, 2)], table_sem.at[1])
    second_half.start()
    second_half.wait()

    run_k[pairs] = jnp.zeros(run_k.shape[1:], jnp.float32)
    run_v[pairs] = jnp.zeros(run_v.shape[1:], jnp.float32)

    for t in range(2):
        for d in order:
            if d == 0:
                in_own(t).wait()
            else:
                in_wait(t, d)
            for way in range(2):
                fwd_copy(t, d, way).start()

    def fwd_wait(t, d, way):
        span = incoming[t][1]
        chunk = source(d)
        pltpu.make_async_remote_copy(
            src_ref=span.at[rows(T, chunk)],
            dst_ref=span.at[rows(2 * T if way == 0 else 0, chunk)],
            send_sem=fwd_send.at[t, d, way], recv_sem=fwd_recv.at[t, d, way],
            device_id={"ctx": ctx_peer[way]}, device_id_type=MESH).wait_recv()

    for t in range(2):
        for d in order:
            for way in range(2):
                fwd_wait(t, d, way)

    low = (lax.broadcasted_iota(jnp.int32, (1, 128), 1) < HEAD_DIM).astype(jnp.float32)
    low_mask = low.astype(jnp.bfloat16)
    high_mask = (1.0 - low).astype(jnp.bfloat16)
    low_lanes = lax.broadcasted_iota(jnp.int32, (BLOCK_TOK, 128), 1) < HEAD_DIM
    exp_scale = scale * math.log2(math.e)

    def one_block(s, turn):
        q = q_loc[s]
        g = g_loc[s]
        wq = jnp.concatenate([q * low_mask, q * high_mask], axis=0)
        wg = jnp.concatenate([g * low_mask, g * high_mask], axis=0)
        places = [table[0, n, turn] for n in range(NBR)]
        ks = jnp.concatenate([k_span[p] for p in places], axis=0)
        vs = jnp.concatenate([v_span[p] for p in places], axis=0)
        scores = lax.dot_general(ks, wq, NT, preferred_element_type=jnp.float32)
        top = jnp.max(scores, axis=0, keepdims=True)
        weights = jnp.exp2((scores - top) * exp_scale)
        inverse = 1.0 / jnp.sum(weights, axis=0, keepdims=True)
        prob = weights * inverse
        grad_prob = lax.dot_general(vs, wg, NT, preferred_element_type=jnp.float32)
        delta = jnp.sum(prob * grad_prob, axis=0, keepdims=True)
        score_low = (prob * (grad_prob - delta)).astype(jnp.bfloat16)
        prob_low = prob.astype(jnp.bfloat16)
        dv = lax.dot_general(prob_low, wg, NN, preferred_element_type=jnp.float32)
        dk = lax.dot_general(score_low, wq, NN, preferred_element_type=jnp.float32)
        dq = lax.dot_general(score_low, ks, TN, preferred_element_type=jnp.float32)
        dq = jnp.where(low_lanes, dq[:BLOCK_TOK], dq[BLOCK_TOK:]) * scale
        dq_stage[s] = dq.astype(jnp.bfloat16)
        for n in range(NBR):
            pair = turn * NBR + n
            before = table[1, n, turn]
            part = slice(n * BLOCK_TOK, (n + 1) * BLOCK_TOK)
            run_k[pair] = dk[part] + run_k[before]
            run_v[pair] = dv[part] + run_v[before]

    def dq_copy(d):
        chunk = source(d)
        return pltpu.make_async_remote_copy(
            src_ref=dq_stage.at[rows(0, chunk)], dst_ref=dq_out.at[:, :, cols(h)],
            send_sem=dq_send.at[d], recv_sem=dq_recv.at[d],
            device_id={"head": chunk}, device_id_type=MESH)

    def dq_own():
        return pltpu.make_async_copy(dq_stage.at[rows(0, h)], dq_out.at[:, :, cols(h)], dq_recv.at[0])

    def one_step(step, carry):
        d = at_step(step, H)
        chunk = source(d)

        @pl.when(step == 0)
        def _():
            in_own(2).wait()
            in_own(3).wait()

        @pl.when(step > 0)
        def _():
            in_wait(2, d)
            in_wait(3, d)

        for k in range(per_chunk):
            one_block(chunk * per_chunk + k, step * per_chunk + k)

        @pl.when(step == 1)
        def _():
            dq_own().start()

        @pl.when(step > 1)
        def _():
            dq_copy(at_step(step - 1, H)).start()

        return carry

    lax.fori_loop(0, H, one_step, 0)
    dq_copy(order[H - 1]).start()

    back_order = order[::-1]

    def ret_copy(d, way, which):
        chunk = peer(d)
        part = (part_k, part_v)[which]
        back = (back_k, back_v)[which]
        return pltpu.make_async_remote_copy(
            src_ref=part.at[rows(way * T, chunk)], dst_ref=back.at[rows(way * T, chunk)],
            send_sem=ret_send.at[which, d, way], recv_sem=ret_recv.at[which, d, way],
            device_id={"ctx": ctx_peer[way]}, device_id_type=MESH)

    for d in back_order:
        chunk = peer(d)
        for way in range(2):
            region = 0 if way == 0 else 2
            for k in range(per_chunk):
                block = chunk * per_chunk + k
                end = table[2, 0, region * per_ctx + block]
                part_k[way * T + block] = (run_k[end] * scale).astype(jnp.bfloat16)
                part_v[way * T + block] = run_v[end].astype(jnp.bfloat16)
        for way in range(2):
            for which in range(2):
                ret_copy(d, way, which).start()

    def out_copy(d, which):
        chunk = peer(d)
        return pltpu.make_async_remote_copy(
            src_ref=(sum_k, sum_v)[which].at[rows(0, chunk)], dst_ref=(dk_out, dv_out)[which].at[:, :, cols(h)],
            send_sem=out_send.at[which, d], recv_sem=out_recv.at[which, d],
            device_id={"head": chunk}, device_id_type=MESH)

    def out_own(which):
        return pltpu.make_async_copy(
            (sum_k, sum_v)[which].at[rows(0, h)], (dk_out, dv_out)[which].at[:, :, cols(h)], out_recv.at[which, 0])

    for d in back_order:
        chunk = peer(d)
        for way in range(2):
            for which in range(2):
                ret_copy(d, way, which).wait_recv()
        for k in range(per_chunk):
            block = chunk * per_chunk + k
            end = table[2, 0, per_ctx + block]
            sum_k[block] = (run_k[end] * scale + back_k[block].astype(jnp.float32)
                            + back_k[T + block].astype(jnp.float32)).astype(jnp.bfloat16)
            sum_v[block] = (run_v[end] + back_v[block].astype(jnp.float32)
                            + back_v[T + block].astype(jnp.float32)).astype(jnp.bfloat16)
        for which in range(2):
            if d == 0:
                out_own(which).start()
            else:
                out_copy(d, which).start()

    dq_own().wait()
    for which in range(2):
        out_own(which).wait()
    for d in order[1:]:
        for t in range(4):
            in_copy(t, d).wait_send()
        dq_copy(d).wait_send()
        pltpu.make_async_remote_copy(
            src_ref=dq_stage.at[rows(0, peer(d))], dst_ref=dq_out.at[:, :, cols(peer(d))],
            send_sem=dq_send.at[d], recv_sem=dq_recv.at[d],
            device_id={"head": peer(d)}, device_id_type=MESH).wait_recv()
        for which in range(2):
            out_copy(d, which).wait_send()
            pltpu.make_async_remote_copy(
                src_ref=(sum_k, sum_v)[which].at[rows(0, source(d))],
                dst_ref=(dk_out, dv_out)[which].at[:, :, cols(source(d))],
                send_sem=out_send.at[which, d], recv_sem=out_recv.at[which, d],
                device_id={"head": source(d)}, device_id_type=MESH).wait_recv()
    for d in order:
        for way in range(2):
            for which in range(2):
                fwd_copy(which, d, way).wait_send()
                ret_copy(d, way, which).wait_send()


def body(queries, key_states, value_states, grad_output, block_slot, neighbours):
    H = lax.axis_size("head")
    C = lax.axis_size("ctx")
    rows, width = queries.shape
    chunk = rows // BLOCK_TOK
    per_ctx = chunk * H
    pairs = per_ctx * NBR
    T = per_ctx
    hbm = pl.BlockSpec(memory_space=pltpu.HBM)
    anywhere = pl.BlockSpec(memory_space=pl.ANY)
    out = jax.ShapeDtypeStruct((chunk, BLOCK_TOK, width), jnp.bfloat16)
    dma = pltpu.SemaphoreType.DMA
    low = jnp.bfloat16
    grads = pl.pallas_call(
        functools.partial(main_kernel, H, C),
        out_shape=(out, out, out),
        in_specs=[hbm] * 6,
        out_specs=(anywhere,) * 3,
        scratch_shapes=[
            pltpu.VMEM((1,) + block_slot.shape, jnp.int32), pltpu.VMEM(neighbours.shape[::-1], jnp.int32),
            pltpu.VMEM((3, NBR, 128), jnp.int32), pltpu.SMEM((3, NBR, 128), jnp.int32), dma((4,)),
            pltpu.VMEM((T, BLOCK_TOK, 128), low), pltpu.VMEM((T, BLOCK_TOK, 128), low),
            pltpu.VMEM((3 * T, BLOCK_TOK, 128), low), pltpu.VMEM((3 * T, BLOCK_TOK, 128), low),
            pltpu.VMEM((pairs + 1, BLOCK_TOK, 128), jnp.float32),
            pltpu.VMEM((pairs + 1, BLOCK_TOK, 128), jnp.float32),
            pltpu.VMEM((T, BLOCK_TOK, 128), low),
            pltpu.VMEM((2 * T, BLOCK_TOK, 128), low), pltpu.VMEM((2 * T, BLOCK_TOK, 128), low),
            pltpu.VMEM((2 * T, BLOCK_TOK, 128), low), pltpu.VMEM((2 * T, BLOCK_TOK, 128), low),
            pltpu.VMEM((T, BLOCK_TOK, 128), low), pltpu.VMEM((T, BLOCK_TOK, 128), low),
            dma((4, H)), dma((4, H)), dma((2, H, 2)), dma((2, H, 2)), dma((H,)), dma((H,)),
            dma((2, H, 2)), dma((2, H, 2)), dma((2, H)), dma((2, H)),
        ],
        compiler_params=pltpu.CompilerParams(collective_id=0, has_side_effects=True, vmem_limit_bytes=24 * 2**20),
        name="attention",
    )(*(pltpu.with_memory_space_constraint(x, pltpu.HBM) for x in (block_slot[None], neighbours.T) + tuple(
        x.reshape(chunk, BLOCK_TOK, width) for x in (queries, key_states, value_states, grad_output))))
    grads = pl.pallas_call(
        copy_kernel,
        out_shape=(out, out, out),
        in_specs=[anywhere] * 3,
        out_specs=(anywhere,) * 3,
        scratch_shapes=[dma((3,))],
        compiler_params=pltpu.CompilerParams(vmem_limit_bytes=4 * 2**20),
        name="results",
    )(*grads)
    return tuple(x.reshape(rows, width) for x in grads)


def solution(mesh):
    tokens = P(("band", "ctx", "head"), None)
    in_specs = (tokens, tokens, tokens, tokens, P("band"), P("band", None))
    return jax.shard_map(body, mesh=mesh, in_specs=in_specs, out_specs=(tokens, tokens, tokens), check_vma=False)
```

```python
import functools
import math

import jax
import jax.numpy as jnp
from jax import lax
from jax.experimental import pallas as pl
from jax.experimental.pallas import tpu as pltpu
from jax.sharding import PartitionSpec as P

HEAD_DIM = 64
BLOCK_TOK = 64
NBR = 8
TILE_BLOCKS = 2
MESH = pl.DeviceIdType.MESH
NT = (((1,), (1,)), ((), ()))
NN = (((1,), (0,)), ((), ()))
TN = (((0,), (0,)), ((), ()))


def at_step(step, H):
    return lax.rem(jnp.where(step % 2 == 1, (step + 1) // 2, H - step // 2), H)


def copy_kernel(*refs):
    half = len(refs) // 2
    copies = [pltpu.make_async_copy(refs[i], refs[half + i], refs[-1].at[i]) for i in range(half)]
    for copy in copies:
        copy.start()
    for copy in copies:
        copy.wait()


def main_kernel(heads, ctx_size, slot_in, nbr_in, q_in, k_in, v_in, g_in, dq_out, dk_out, dv_out,
                slot_ref, nbr_ref, table_vec, table, table_sem,
                q_loc, g_loc, k_span, v_span, run_k, run_v, dq_stage, part_k, part_v, back_k, back_v, sum_k, sum_v,
                score_buf, grad_buf, weight_buf, mixed_buf, top_buf, stat_buf,
                in_send, in_recv, fwd_send, fwd_recv, dq_send, dq_recv, ret_send, ret_recv, out_send, out_recv):
    H = heads
    h = lax.axis_index("head")
    c = lax.axis_index("ctx")
    per_chunk = q_in.shape[0]
    T = H * per_chunk
    per_ctx = T
    pairs = per_ctx * NBR
    scale = HEAD_DIM ** -0.5
    ctx_prev = lax.rem(c + ctx_size - 1, ctx_size)
    ctx_next = lax.rem(c + 1, ctx_size)
    ctx_peer = (ctx_prev, ctx_next)

    def peer(d):
        return lax.rem(h + d, H)

    def source(d):
        return lax.rem(h + H - d, H)

    def rows(base, chunk):
        return pl.ds(base + chunk * per_chunk, per_chunk)

    def cols(chunk):
        return pl.ds(pl.multiple_of(chunk * 128, 128), 128)

    slot_copy = pltpu.make_async_copy(slot_in, slot_ref, table_sem.at[2])
    nbr_copy = pltpu.make_async_copy(nbr_in, nbr_ref, table_sem.at[3])
    slot_copy.start()
    nbr_copy.start()
    barrier = pltpu.get_barrier_semaphore()
    for d in range(1, H):
        pl.semaphore_signal(barrier, inc=1, device_id={"head": peer(d)}, device_id_type=MESH)
    for p in ctx_peer:
        pl.semaphore_signal(barrier, inc=1, device_id={"ctx": p}, device_id_type=MESH)
    pl.semaphore_wait(barrier, H + 1)

    order = [0]
    for step in range(1, H):
        order.append(((step + 1) // 2 if step % 2 else H - step // 2) % H)

    incoming = ((k_in, k_span, T), (v_in, v_span, T), (q_in, q_loc, 0), (g_in, g_loc, 0))

    def in_copy(t, d):
        src, dst, base = incoming[t]
        return pltpu.make_async_remote_copy(
            src_ref=src.at[:, :, cols(peer(d))], dst_ref=dst.at[rows(base, h)],
            send_sem=in_send.at[t, d], recv_sem=in_recv.at[t, d],
            device_id={"head": peer(d)}, device_id_type=MESH)

    def in_own(t):
        src, dst, base = incoming[t]
        return pltpu.make_async_copy(src.at[:, :, cols(h)], dst.at[rows(base, h)], in_recv.at[t, 0])

    def in_wait(t, d):
        src, dst, base = incoming[t]
        pltpu.make_async_remote_copy(
            src_ref=src.at[:, :, cols(peer(d))], dst_ref=dst.at[rows(base, source(d))],
            send_sem=in_send.at[t, d], recv_sem=in_recv.at[t, d],
            device_id={"head": peer(d)}, device_id_type=MESH).wait_recv()

    for t in range(4):
        in_own(t).start()
        for d in order[1:]:
            in_copy(t, d).start()

    def fwd_copy(t, d, way):
        span = incoming[t][1]
        chunk = source(d)
        return pltpu.make_async_remote_copy(
            src_ref=span.at[rows(T, chunk)],
            dst_ref=span.at[rows(2 * T if way == 0 else 0, chunk)],
            send_sem=fwd_send.at[t, d, way], recv_sem=fwd_recv.at[t, d, way],
            device_id={"ctx": ctx_peer[way]}, device_id_type=MESH)

    slot_copy.wait()
    nbr_copy.wait()
    slots = slot_ref.shape[1]
    slot_row = slot_ref[...]
    nbr = nbr_ref[...]
    slot_lane = lax.broadcasted_iota(jnp.int32, (NBR, slots), 1)
    lane = lax.broadcasted_iota(jnp.int32, (NBR, 128), 1)
    own = lane * NBR + lax.broadcasted_iota(jnp.int32, (NBR, 128), 0)
    targets = jnp.zeros((NBR, 128), jnp.int32)
    for turn in range(per_ctx):
        s = source(order[turn // per_chunk]) * per_chunk + turn % per_chunk
        near = jnp.sum(jnp.where(slot_row == c * per_ctx + s, nbr, 0), axis=1, keepdims=True)
        slot = jnp.sum(jnp.where(slot_lane == near, slot_row, 0), axis=1, keepdims=True)
        target = jnp.zeros_like(slot)
        for region, owner in enumerate((ctx_prev, c, ctx_next)):
            local = slot - owner * per_ctx
            target = jnp.where((local >= 0) & (local < per_ctx), local + region * per_ctx, target)
        targets = jnp.where(lane == turn, target, targets)
    table_vec[0] = targets
    first_half = pltpu.make_async_copy(table_vec.at[pl.ds(0, 1)], table.at[pl.ds(0, 1)], table_sem.at[0])
    first_half.start()
    first_half.wait()

    def chain(turn, carry):
        before, last = carry
        for n in range(NBR):
            target = table[0, n, turn]
            pair = turn * NBR + n
            before = jnp.where((targets == target) & (own > pair), pair, before)
            last = jnp.where(lane == target, pair, last)
        return before, last

    nothing = jnp.full((NBR, 128), pairs, jnp.int32)
    before, last = lax.fori_loop(0, per_ctx, chain, (nothing, nothing))
    table_vec[1] = before
    table_vec[2] = last
    second_half = pltpu.make_async_copy(table_vec.at[pl.ds(1, 2)], table.at[pl.ds(1, 2)], table_sem.at[1])
    second_half.start()
    second_half.wait()

    run_k[pairs] = jnp.zeros(run_k.shape[1:], jnp.float32)
    run_v[pairs] = jnp.zeros(run_v.shape[1:], jnp.float32)

    for t in range(2):
        for d in order:
            if d == 0:
                in_own(t).wait()
            else:
                in_wait(t, d)
            for way in range(2):
                fwd_copy(t, d, way).start()

    def fwd_wait(t, d, way):
        span = incoming[t][1]
        chunk = source(d)
        pltpu.make_async_remote_copy(
            src_ref=span.at[rows(T, chunk)],
            dst_ref=span.at[rows(2 * T if way == 0 else 0, chunk)],
            send_sem=fwd_send.at[t, d, way], recv_sem=fwd_recv.at[t, d, way],
            device_id={"ctx": ctx_peer[way]}, device_id_type=MESH).wait_recv()

    for t in range(2):
        for d in order:
            for way in range(2):
                fwd_wait(t, d, way)

    low = (lax.broadcasted_iota(jnp.int32, (1, 128), 1) < HEAD_DIM).astype(jnp.float32)
    low_mask = low.astype(jnp.bfloat16)
    high_mask = (1.0 - low).astype(jnp.bfloat16)
    low_lanes = lax.broadcasted_iota(jnp.int32, (BLOCK_TOK, 128), 1) < HEAD_DIM
    exp_scale = scale * math.log2(math.e)

    tile = TILE_BLOCKS * BLOCK_TOK
    tiles = NBR // TILE_BLOCKS

    def slot_at(turn):
        step = turn // per_chunk
        return source(at_step(step, H)) * per_chunk + turn % per_chunk

    def diagonal(x):
        return jnp.concatenate([x * low_mask, x * high_mask], axis=0)

    def listed(span, turn, r):
        return jnp.concatenate([span[table[0, r * TILE_BLOCKS + n, turn]] for n in range(TILE_BLOCKS)], axis=0)

    def fold(x):
        return x.reshape(tile // 8, 8, 128)

    class Scores:
        def __init__(self, turn, side):
            self.turn, self.side = turn, side
            s = slot_at(turn)
            self.wq, self.wg = diagonal(q_loc[s]), diagonal(g_loc[s])
            self.top = None

        def tile(self, r):
            part = pl.ds(r * tile, tile)
            scores = lax.dot_general(listed(k_span, self.turn, r), self.wq, NT, preferred_element_type=jnp.float32)
            score_buf[self.side, part, :] = scores
            top = jnp.max(fold(scores), axis=0)
            self.top = top if self.top is None else jnp.maximum(self.top, top)
            grad_buf[self.side, part, :] = lax.dot_general(
                listed(v_span, self.turn, r), self.wg, NT, preferred_element_type=jnp.float32)

        def finish(self):
            top_buf[self.side] = self.top

    class Weights:
        def __init__(self, turn, side):
            self.side = side
            self.top = jnp.max(top_buf[side], axis=0, keepdims=True)
            self.total = self.mixed = None

        def tile(self, r):
            part = pl.ds(r * tile, tile)
            weights = jnp.exp2((score_buf[self.side, part, :] - self.top) * exp_scale)
            mixed = weights * grad_buf[self.side, part, :]
            weight_buf[self.side, part, :] = weights
            mixed_buf[self.side, part, :] = mixed
            total, mixed = jnp.sum(fold(weights), axis=0), jnp.sum(fold(mixed), axis=0)
            self.total = total if self.total is None else self.total + total
            self.mixed = mixed if self.mixed is None else self.mixed + mixed

        def finish(self):
            inverse = 1.0 / jnp.sum(self.total, axis=0, keepdims=True)
            stat_buf[self.side, 0:1, :] = inverse
            stat_buf[self.side, 1:2, :] = jnp.sum(self.mixed, axis=0, keepdims=True) * inverse

    class Gradients:
        def __init__(self, turn, side):
            self.turn, self.side = turn, side
            self.slot = slot_at(turn)
            self.wq, self.wg = diagonal(q_loc[self.slot]), diagonal(g_loc[self.slot])
            self.inverse, self.delta = stat_buf[side, 0:1, :], stat_buf[side, 1:2, :]
            self.dq = None

        def tile(self, r):
            part = pl.ds(r * tile, tile)
            prob = weight_buf[self.side, part, :] * self.inverse
            score_low = (mixed_buf[self.side, part, :] * self.inverse - prob * self.delta).astype(jnp.bfloat16)
            prob_low = prob.astype(jnp.bfloat16)
            dv = lax.dot_general(prob_low, self.wg, NN, preferred_element_type=jnp.float32)
            dk = lax.dot_general(score_low, self.wq, NN, preferred_element_type=jnp.float32)
            dq = lax.dot_general(score_low, listed(k_span, self.turn, r), TN, preferred_element_type=jnp.float32)
            self.dq = dq if self.dq is None else self.dq + dq
            for k in range(TILE_BLOCKS):
                n = r * TILE_BLOCKS + k
                pair = self.turn * NBR + n
                before = table[1, n, self.turn]
                here = slice(k * BLOCK_TOK, (k + 1) * BLOCK_TOK)
                run_k[pair] = dk[here] + run_k[before]
                run_v[pair] = dv[here] + run_v[before]

        def finish(self):
            dq = jnp.where(low_lanes, self.dq[:BLOCK_TOK], self.dq[BLOCK_TOK:]) * scale
            dq_stage[self.slot] = dq.astype(jnp.bfloat16)

    def together(*stages):
        for r in range(tiles):
            for stage in stages:
                stage.tile(r)
        for stage in stages:
            stage.finish()

    def dq_copy(d):
        chunk = source(d)
        return pltpu.make_async_remote_copy(
            src_ref=dq_stage.at[rows(0, chunk)], dst_ref=dq_out.at[:, :, cols(h)],
            send_sem=dq_send.at[d], recv_sem=dq_recv.at[d],
            device_id={"head": chunk}, device_id_type=MESH)

    def dq_own():
        return pltpu.make_async_copy(dq_stage.at[rows(0, h)], dq_out.at[:, :, cols(h)], dq_recv.at[0])

    in_own(2).wait()
    in_own(3).wait()
    together(Scores(0, 0))
    together(Weights(0, 0), Scores(1, 1))

    def one_step(step, carry):
        d = at_step(step, H)
        in_wait(2, d)
        in_wait(3, d)

        @pl.when(step == 2)
        def _():
            dq_own().start()

        @pl.when(step > 2)
        def _():
            dq_copy(at_step(step - 2, H)).start()

        turn = step * per_chunk
        together(Gradients(turn - 2, 0), Weights(turn - 1, 1), Scores(turn, 0))
        together(Gradients(turn - 1, 1), Weights(turn, 0), Scores(turn + 1, 1))
        return carry

    lax.fori_loop(1, H, one_step, 0)
    if H == 2:
        dq_own().start()
    else:
        dq_copy(order[H - 2]).start()
    turn = H * per_chunk
    together(Gradients(turn - 2, 0), Weights(turn - 1, 1))
    together(Gradients(turn - 1, 1))
    dq_copy(order[H - 1]).start()

    back_order = order[::-1]

    def ret_copy(d, way, which):
        chunk = peer(d)
        part = (part_k, part_v)[which]
        back = (back_k, back_v)[which]
        return pltpu.make_async_remote_copy(
            src_ref=part.at[rows(way * T, chunk)], dst_ref=back.at[rows(way * T, chunk)],
            send_sem=ret_send.at[which, d, way], recv_sem=ret_recv.at[which, d, way],
            device_id={"ctx": ctx_peer[way]}, device_id_type=MESH)

    for d in back_order:
        chunk = peer(d)
        for way in range(2):
            region = 0 if way == 0 else 2
            for k in range(per_chunk):
                block = chunk * per_chunk + k
                end = table[2, 0, region * per_ctx + block]
                part_k[way * T + block] = (run_k[end] * scale).astype(jnp.bfloat16)
                part_v[way * T + block] = run_v[end].astype(jnp.bfloat16)
        for way in range(2):
            for which in range(2):
                ret_copy(d, way, which).start()

    def out_copy(d, which):
        chunk = peer(d)
        return pltpu.make_async_remote_copy(
            src_ref=(sum_k, sum_v)[which].at[rows(0, chunk)], dst_ref=(dk_out, dv_out)[which].at[:, :, cols(h)],
            send_sem=out_send.at[which, d], recv_sem=out_recv.at[which, d],
            device_id={"head": chunk}, device_id_type=MESH)

    def out_own(which):
        return pltpu.make_async_copy(
            (sum_k, sum_v)[which].at[rows(0, h)], (dk_out, dv_out)[which].at[:, :, cols(h)], out_recv.at[which, 0])

    for d in back_order:
        chunk = peer(d)
        for way in range(2):
            for which in range(2):
                ret_copy(d, way, which).wait_recv()
        for k in range(per_chunk):
            block = chunk * per_chunk + k
            end = table[2, 0, per_ctx + block]
            sum_k[block] = (run_k[end] * scale + back_k[block].astype(jnp.float32)
                            + back_k[T + block].astype(jnp.float32)).astype(jnp.bfloat16)
            sum_v[block] = (run_v[end] + back_v[block].astype(jnp.float32)
                            + back_v[T + block].astype(jnp.float32)).astype(jnp.bfloat16)
        for which in range(2):
            if d == 0:
                out_own(which).start()
            else:
                out_copy(d, which).start()

    dq_own().wait()
    for which in range(2):
        out_own(which).wait()
    for d in order[1:]:
        for t in range(4):
            in_copy(t, d).wait_send()
        dq_copy(d).wait_send()
        pltpu.make_async_remote_copy(
            src_ref=dq_stage.at[rows(0, peer(d))], dst_ref=dq_out.at[:, :, cols(peer(d))],
            send_sem=dq_send.at[d], recv_sem=dq_recv.at[d],
            device_id={"head": peer(d)}, device_id_type=MESH).wait_recv()
        for which in range(2):
            out_copy(d, which).wait_send()
            pltpu.make_async_remote_copy(
                src_ref=(sum_k, sum_v)[which].at[rows(0, source(d))],
                dst_ref=(dk_out, dv_out)[which].at[:, :, cols(source(d))],
                send_sem=out_send.at[which, d], recv_sem=out_recv.at[which, d],
                device_id={"head": source(d)}, device_id_type=MESH).wait_recv()
    for d in order:
        for way in range(2):
            for which in range(2):
                fwd_copy(which, d, way).wait_send()
                ret_copy(d, way, which).wait_send()


def body(queries, key_states, value_states, grad_output, block_slot, neighbours):
    H = lax.axis_size("head")
    C = lax.axis_size("ctx")
    rows, width = queries.shape
    chunk = rows // BLOCK_TOK
    per_ctx = chunk * H
    pairs = per_ctx * NBR
    T = per_ctx
    hbm = pl.BlockSpec(memory_space=pltpu.HBM)
    anywhere = pl.BlockSpec(memory_space=pl.ANY)
    out = jax.ShapeDtypeStruct((chunk, BLOCK_TOK, width), jnp.bfloat16)
    dma = pltpu.SemaphoreType.DMA
    low = jnp.bfloat16
    grads = pl.pallas_call(
        functools.partial(main_kernel, H, C),
        out_shape=(out, out, out),
        in_specs=[hbm] * 6,
        out_specs=(anywhere,) * 3,
        scratch_shapes=[
            pltpu.VMEM((1,) + block_slot.shape, jnp.int32), pltpu.VMEM(neighbours.shape[::-1], jnp.int32),
            pltpu.VMEM((3, NBR, 128), jnp.int32), pltpu.SMEM((3, NBR, 128), jnp.int32), dma((4,)),
            pltpu.VMEM((T, BLOCK_TOK, 128), low), pltpu.VMEM((T, BLOCK_TOK, 128), low),
            pltpu.VMEM((3 * T, BLOCK_TOK, 128), low), pltpu.VMEM((3 * T, BLOCK_TOK, 128), low),
            pltpu.VMEM((pairs + 1, BLOCK_TOK, 128), jnp.float32),
            pltpu.VMEM((pairs + 1, BLOCK_TOK, 128), jnp.float32),
            pltpu.VMEM((T, BLOCK_TOK, 128), low),
            pltpu.VMEM((2 * T, BLOCK_TOK, 128), low), pltpu.VMEM((2 * T, BLOCK_TOK, 128), low),
            pltpu.VMEM((2 * T, BLOCK_TOK, 128), low), pltpu.VMEM((2 * T, BLOCK_TOK, 128), low),
            pltpu.VMEM((T, BLOCK_TOK, 128), low), pltpu.VMEM((T, BLOCK_TOK, 128), low),
            *[pltpu.VMEM((2, NBR * BLOCK_TOK, 128), jnp.float32)] * 4,
            pltpu.VMEM((2, 8, 128), jnp.float32), pltpu.VMEM((2, 8, 128), jnp.float32),
            dma((4, H)), dma((4, H)), dma((2, H, 2)), dma((2, H, 2)), dma((H,)), dma((H,)),
            dma((2, H, 2)), dma((2, H, 2)), dma((2, H)), dma((2, H)),
        ],
        compiler_params=pltpu.CompilerParams(collective_id=0, has_side_effects=True, vmem_limit_bytes=24 * 2**20),
        name="attention",
    )(*(pltpu.with_memory_space_constraint(x, pltpu.HBM) for x in (block_slot[None], neighbours.T) + tuple(
        x.reshape(chunk, BLOCK_TOK, width) for x in (queries, key_states, value_states, grad_output))))
    grads = pl.pallas_call(
        copy_kernel,
        out_shape=(out, out, out),
        in_specs=[anywhere] * 3,
        out_specs=(anywhere,) * 3,
        scratch_shapes=[dma((3,))],
        compiler_params=pltpu.CompilerParams(vmem_limit_bytes=4 * 2**20),
        name="results",
    )(*grads)
    return tuple(x.reshape(rows, width) for x in grads)


def solution(mesh):
    tokens = P(("band", "ctx", "head"), None)
    in_specs = (tokens, tokens, tokens, tokens, P("band"), P("band", None))
    return jax.shard_map(body, mesh=mesh, in_specs=in_specs, out_specs=(tokens, tokens, tokens), check_vma=False)
```

```python
import functools
import math

import jax
import jax.numpy as jnp
from jax import lax
from jax.experimental import pallas as pl
from jax.experimental.pallas import tpu as pltpu
from jax.sharding import PartitionSpec as P

HEAD_DIM = 64
BLOCK_TOK = 64
NBR = 8
TILE_BLOCKS = 8
MESH = pl.DeviceIdType.MESH
NT = (((1,), (1,)), ((), ()))
NN = (((1,), (0,)), ((), ()))
TN = (((0,), (0,)), ((), ()))


def at_step(step, H):
    return lax.rem(jnp.where(step % 2 == 1, (step + 1) // 2, H - step // 2), H)


def copy_kernel(*refs):
    half = len(refs) // 2
    parts = [(i, k) for i in range(half) for k in range(refs[i].shape[0])]
    copies = [pltpu.make_async_copy(refs[i].at[k], refs[half + i].at[k], refs[-1].at[i, k]) for i, k in parts]
    for copy in copies:
        copy.start()
    for copy in copies:
        copy.wait()


def main_kernel(heads, ctx_size, slot_in, nbr_in, q_in, k_in, v_in, g_in, dq_out, dk_out, dv_out,
                slot_ref, nbr_ref, table_vec, table, table_sem,
                q_loc, g_loc, k_span, v_span, run_k, run_v, dq_stage, part_k, part_v, back_k, back_v, sum_k, sum_v,
                score_buf, weight_buf, mixed_buf, top_buf, total_buf, stat_buf,
                in_send, in_recv, fwd_send, fwd_recv, dq_send, dq_recv, ret_send, ret_recv, out_send, out_recv):
    H = heads
    h = lax.axis_index("head")
    c = lax.axis_index("ctx")
    per_chunk = q_in.shape[0]
    T = H * per_chunk
    per_ctx = T
    pairs = per_ctx * NBR
    scale = HEAD_DIM ** -0.5
    ctx_prev = lax.rem(c + ctx_size - 1, ctx_size)
    ctx_next = lax.rem(c + 1, ctx_size)
    ctx_peer = (ctx_prev, ctx_next)

    def peer(d):
        return lax.rem(h + d, H)

    def source(d):
        return lax.rem(h + H - d, H)

    def rows(base, chunk):
        return pl.ds(base + chunk * per_chunk, per_chunk)

    def cols(chunk):
        return pl.ds(pl.multiple_of(chunk * 128, 128), 128)

    slot_copy = pltpu.make_async_copy(slot_in, slot_ref, table_sem.at[2])
    nbr_copy = pltpu.make_async_copy(nbr_in, nbr_ref, table_sem.at[3])
    slot_copy.start()
    nbr_copy.start()
    barrier = pltpu.get_barrier_semaphore()
    for d in range(1, H):
        pl.semaphore_signal(barrier, inc=1, device_id={"head": peer(d)}, device_id_type=MESH)
    for p in ctx_peer:
        pl.semaphore_signal(barrier, inc=1, device_id={"ctx": p}, device_id_type=MESH)
    pl.semaphore_wait(barrier, H + 1)

    order = [0]
    for step in range(1, H):
        order.append(((step + 1) // 2 if step % 2 else H - step // 2) % H)

    incoming = ((k_in, k_span, T), (q_in, q_loc, 0), (v_in, v_span, T), (g_in, g_loc, 0))

    def in_copy(t, d):
        src, dst, base = incoming[t]
        return pltpu.make_async_remote_copy(
            src_ref=src.at[:, :, cols(peer(d))], dst_ref=dst.at[rows(base, h)],
            send_sem=in_send.at[t, d], recv_sem=in_recv.at[t, d],
            device_id={"head": peer(d)}, device_id_type=MESH)

    def in_own(t):
        src, dst, base = incoming[t]
        return pltpu.make_async_copy(src.at[:, :, cols(h)], dst.at[rows(base, h)], in_recv.at[t, 0])

    def in_wait(t, d):
        src, dst, base = incoming[t]
        pltpu.make_async_remote_copy(
            src_ref=src.at[:, :, cols(peer(d))], dst_ref=dst.at[rows(base, source(d))],
            send_sem=in_send.at[t, d], recv_sem=in_recv.at[t, d],
            device_id={"head": peer(d)}, device_id_type=MESH).wait_recv()

    for t in range(4):
        in_own(t).start()
        for d in order[1:]:
            in_copy(t, d).start()

    def fwd_copy(t, d, way):
        span = incoming[2 * t][1]
        chunk = source(d)
        return pltpu.make_async_remote_copy(
            src_ref=span.at[rows(T, chunk)],
            dst_ref=span.at[rows(2 * T if way == 0 else 0, chunk)],
            send_sem=fwd_send.at[t, d, way], recv_sem=fwd_recv.at[t, d, way],
            device_id={"ctx": ctx_peer[way]}, device_id_type=MESH)

    slot_copy.wait()
    nbr_copy.wait()
    slots = slot_ref.shape[1]
    slot_row = slot_ref[...]
    nbr = nbr_ref[...]
    slot_lane = lax.broadcasted_iota(jnp.int32, (NBR, slots), 1)
    lane = lax.broadcasted_iota(jnp.int32, (NBR, 128), 1)
    own = lane * NBR + lax.broadcasted_iota(jnp.int32, (NBR, 128), 0)
    targets = jnp.zeros((NBR, 128), jnp.int32)
    for turn in range(per_ctx):
        s = source(order[turn // per_chunk]) * per_chunk + turn % per_chunk
        near = jnp.sum(jnp.where(slot_row == c * per_ctx + s, nbr, 0), axis=1, keepdims=True)
        slot = jnp.sum(jnp.where(slot_lane == near, slot_row, 0), axis=1, keepdims=True)
        target = jnp.zeros_like(slot)
        for region, owner in enumerate((ctx_prev, c, ctx_next)):
            local = slot - owner * per_ctx
            target = jnp.where((local >= 0) & (local < per_ctx), local + region * per_ctx, target)
        targets = jnp.where(lane == turn, target, targets)
    table_vec[0] = targets
    first_half = pltpu.make_async_copy(table_vec.at[pl.ds(0, 1)], table.at[pl.ds(0, 1)], table_sem.at[0])
    first_half.start()
    first_half.wait()

    def chain(turn, carry):
        before, last = carry
        for n in range(NBR):
            target = table[0, n, turn]
            pair = turn * NBR + n
            before = jnp.where((targets == target) & (own > pair), pair, before)
            last = jnp.where(lane == target, pair, last)
        return before, last

    nothing = jnp.full((NBR, 128), pairs, jnp.int32)
    before, last = lax.fori_loop(0, per_ctx, chain, (nothing, nothing))
    table_vec[1] = before
    table_vec[2] = last
    second_half = pltpu.make_async_copy(table_vec.at[pl.ds(1, 2)], table.at[pl.ds(1, 2)], table_sem.at[1])
    second_half.start()
    second_half.wait()

    run_k[pairs] = jnp.zeros(run_k.shape[1:], jnp.float32)
    run_v[pairs] = jnp.zeros(run_v.shape[1:], jnp.float32)

    for d in order:
        if d == 0:
            in_own(0).wait()
        else:
            in_wait(0, d)
        for way in range(2):
            fwd_copy(0, d, way).start()

    def fwd_wait(t, d, way):
        span = incoming[2 * t][1]
        chunk = source(d)
        pltpu.make_async_remote_copy(
            src_ref=span.at[rows(T, chunk)],
            dst_ref=span.at[rows(2 * T if way == 0 else 0, chunk)],
            send_sem=fwd_send.at[t, d, way], recv_sem=fwd_recv.at[t, d, way],
            device_id={"ctx": ctx_peer[way]}, device_id_type=MESH).wait_recv()

    def span_wait(t):
        for d in order:
            for way in range(2):
                fwd_wait(t, d, way)

    span_wait(0)

    low = (lax.broadcasted_iota(jnp.int32, (1, 128), 1) < HEAD_DIM).astype(jnp.float32)
    low_mask = low.astype(jnp.bfloat16)
    high_mask = (1.0 - low).astype(jnp.bfloat16)
    low_lanes = lax.broadcasted_iota(jnp.int32, (BLOCK_TOK, 128), 1) < HEAD_DIM
    exp_scale = scale * math.log2(math.e)

    tile = TILE_BLOCKS * BLOCK_TOK
    tiles = NBR // TILE_BLOCKS

    def slot_at(turn):
        step = turn // per_chunk
        return source(at_step(step, H)) * per_chunk + turn % per_chunk

    def diagonal(x):
        return jnp.concatenate([x * low_mask, x * high_mask], axis=0)

    def listed(span, turn, r):
        return jnp.concatenate([span[table[0, r * TILE_BLOCKS + n, turn]] for n in range(TILE_BLOCKS)], axis=0)

    def fold(x):
        return x.reshape(tile // 8, 8, 128)

    class Scores:
        def __init__(self, turn, side):
            self.turn, self.side = turn, side
            self.wq = diagonal(q_loc[slot_at(turn)])
            self.top = None

        def tile(self, r):
            part = pl.ds(r * tile, tile)
            scores = lax.dot_general(listed(k_span, self.turn, r), self.wq, NT, preferred_element_type=jnp.float32)
            score_buf[self.side, part, :] = scores
            top = jnp.max(fold(scores), axis=0)
            self.top = top if self.top is None else jnp.maximum(self.top, top)

        def finish(self):
            top_buf[self.side] = self.top

    class Weights:
        def __init__(self, turn, side):
            self.turn, self.side = turn, side
            self.top = jnp.max(top_buf[side], axis=0, keepdims=True)
            self.total = None

        def tile(self, r):
            part = pl.ds(r * tile, tile)
            weights = jnp.exp2((score_buf[self.side, part, :] - self.top) * exp_scale)
            weight_buf[self.turn, part, :] = weights
            total = jnp.sum(fold(weights), axis=0)
            self.total = total if self.total is None else self.total + total

        def finish(self):
            total_buf[self.turn] = self.total

    class Mixed:
        def __init__(self, turn, side):
            self.turn, self.side = turn, side
            self.wg = diagonal(g_loc[slot_at(turn)])
            self.mixed = None

        def tile(self, r):
            part = pl.ds(r * tile, tile)
            grad = lax.dot_general(listed(v_span, self.turn, r), self.wg, NT, preferred_element_type=jnp.float32)
            mixed = weight_buf[self.turn, part, :] * grad
            mixed_buf[self.side, part, :] = mixed
            mixed = jnp.sum(fold(mixed), axis=0)
            self.mixed = mixed if self.mixed is None else self.mixed + mixed

        def finish(self):
            stat_buf[self.side] = self.mixed

    class Gradients:
        def __init__(self, turn, side):
            self.turn, self.side = turn, side
            self.slot = slot_at(turn)
            self.wq, self.wg = diagonal(q_loc[self.slot]), diagonal(g_loc[self.slot])
            self.inverse = 1.0 / jnp.sum(total_buf[turn], axis=0, keepdims=True)
            self.delta = jnp.sum(stat_buf[side], axis=0, keepdims=True) * self.inverse
            self.dq = None

        def tile(self, r):
            part = pl.ds(r * tile, tile)
            prob = weight_buf[self.turn, part, :] * self.inverse
            score_low = (mixed_buf[self.side, part, :] * self.inverse - prob * self.delta).astype(jnp.bfloat16)
            prob_low = prob.astype(jnp.bfloat16)
            dv = lax.dot_general(prob_low, self.wg, NN, preferred_element_type=jnp.float32)
            dk = lax.dot_general(score_low, self.wq, NN, preferred_element_type=jnp.float32)
            dq = lax.dot_general(score_low, listed(k_span, self.turn, r), TN, preferred_element_type=jnp.float32)
            self.dq = dq if self.dq is None else self.dq + dq
            for k in range(TILE_BLOCKS):
                n = r * TILE_BLOCKS + k
                pair = self.turn * NBR + n
                before = table[1, n, self.turn]
                here = slice(k * BLOCK_TOK, (k + 1) * BLOCK_TOK)
                run_k[pair] = dk[here] + run_k[before]
                run_v[pair] = dv[here] + run_v[before]

        def finish(self):
            dq = jnp.where(low_lanes, self.dq[:BLOCK_TOK], self.dq[BLOCK_TOK:]) * scale
            dq_stage[self.slot] = dq.astype(jnp.bfloat16)

    def together(*stages):
        for r in range(tiles):
            for stage in stages:
                stage.tile(r)
        for stage in stages:
            stage.finish()

    def dq_copy(d):
        chunk = source(d)
        return pltpu.make_async_remote_copy(
            src_ref=dq_stage.at[rows(0, chunk)], dst_ref=dq_out.at[:, :, cols(h)],
            send_sem=dq_send.at[d], recv_sem=dq_recv.at[d],
            device_id={"head": chunk}, device_id_type=MESH)

    def dq_own():
        return pltpu.make_async_copy(dq_stage.at[rows(0, h)], dq_out.at[:, :, cols(h)], dq_recv.at[0])

    turns = H * per_chunk
    in_own(2).wait()
    for way in range(2):
        fwd_copy(1, 0, way).start()
    in_own(1).wait()
    together(Scores(0, 0))
    together(Weights(0, 0), Scores(1, 1))

    def first_step(step, carry):
        d = at_step(step, H)
        in_wait(1, d)
        turn = step * per_chunk
        together(Weights(turn - 1, 1), Scores(turn, 0))
        together(Weights(turn, 0), Scores(turn + 1, 1))
        in_wait(2, d)
        for way in range(2):
            fwd_copy(1, d, way).start()
        return carry

    lax.fori_loop(1, H, first_step, 0)
    together(Weights(turns - 1, 1))

    span_wait(1)
    in_own(3).wait()
    together(Mixed(0, 0))
    together(Gradients(0, 0), Mixed(1, 1))

    def second_step(step, carry):
        in_wait(3, at_step(step, H))

        @pl.when(step == 2)
        def _():
            dq_own().start()

        @pl.when(step > 2)
        def _():
            dq_copy(at_step(step - 2, H)).start()

        turn = step * per_chunk
        together(Gradients(turn - 1, 1), Mixed(turn, 0))
        together(Gradients(turn, 0), Mixed(turn + 1, 1))
        return carry

    lax.fori_loop(1, H, second_step, 0)
    if H == 2:
        dq_own().start()
    else:
        dq_copy(order[H - 2]).start()
    together(Gradients(turns - 1, 1))
    dq_copy(order[H - 1]).start()

    back_order = order[::-1]

    def ret_copy(d, way, which):
        chunk = peer(d)
        part = (part_k, part_v)[which]
        back = (back_k, back_v)[which]
        return pltpu.make_async_remote_copy(
            src_ref=part.at[rows(way * T, chunk)], dst_ref=back.at[rows(way * T, chunk)],
            send_sem=ret_send.at[which, d, way], recv_sem=ret_recv.at[which, d, way],
            device_id={"ctx": ctx_peer[way]}, device_id_type=MESH)

    for d in back_order:
        chunk = peer(d)
        for way in range(2):
            region = 0 if way == 0 else 2
            for k in range(per_chunk):
                block = chunk * per_chunk + k
                end = table[2, 0, region * per_ctx + block]
                part_k[way * T + block] = (run_k[end] * scale).astype(jnp.bfloat16)
                part_v[way * T + block] = run_v[end].astype(jnp.bfloat16)
        for way in range(2):
            for which in range(2):
                ret_copy(d, way, which).start()

    def out_copy(d, which):
        chunk = peer(d)
        return pltpu.make_async_remote_copy(
            src_ref=(sum_k, sum_v)[which].at[rows(0, chunk)], dst_ref=(dk_out, dv_out)[which].at[:, :, cols(h)],
            send_sem=out_send.at[which, d], recv_sem=out_recv.at[which, d],
            device_id={"head": chunk}, device_id_type=MESH)

    def out_own(which):
        return pltpu.make_async_copy(
            (sum_k, sum_v)[which].at[rows(0, h)], (dk_out, dv_out)[which].at[:, :, cols(h)], out_recv.at[which, 0])

    for d in back_order:
        chunk = peer(d)
        for way in range(2):
            for which in range(2):
                ret_copy(d, way, which).wait_recv()
        for k in range(per_chunk):
            block = chunk * per_chunk + k
            end = table[2, 0, per_ctx + block]
            sum_k[block] = (run_k[end] * scale + back_k[block].astype(jnp.float32)
                            + back_k[T + block].astype(jnp.float32)).astype(jnp.bfloat16)
            sum_v[block] = (run_v[end] + back_v[block].astype(jnp.float32)
                            + back_v[T + block].astype(jnp.float32)).astype(jnp.bfloat16)
        for which in range(2):
            if d == 0:
                out_own(which).start()
            else:
                out_copy(d, which).start()

    dq_own().wait()
    for which in range(2):
        out_own(which).wait()
    for d in order[1:]:
        for t in range(4):
            in_copy(t, d).wait_send()
        dq_copy(d).wait_send()
        pltpu.make_async_remote_copy(
            src_ref=dq_stage.at[rows(0, peer(d))], dst_ref=dq_out.at[:, :, cols(peer(d))],
            send_sem=dq_send.at[d], recv_sem=dq_recv.at[d],
            device_id={"head": peer(d)}, device_id_type=MESH).wait_recv()
        for which in range(2):
            out_copy(d, which).wait_send()
            pltpu.make_async_remote_copy(
                src_ref=(sum_k, sum_v)[which].at[rows(0, source(d))],
                dst_ref=(dk_out, dv_out)[which].at[:, :, cols(source(d))],
                send_sem=out_send.at[which, d], recv_sem=out_recv.at[which, d],
                device_id={"head": source(d)}, device_id_type=MESH).wait_recv()
    for d in order:
        for way in range(2):
            for which in range(2):
                fwd_copy(which, d, way).wait_send()
                ret_copy(d, way, which).wait_send()


def body(queries, key_states, value_states, grad_output, block_slot, neighbours):
    H = lax.axis_size("head")
    C = lax.axis_size("ctx")
    rows, width = queries.shape
    chunk = rows // BLOCK_TOK
    per_ctx = chunk * H
    pairs = per_ctx * NBR
    T = per_ctx
    hbm = pl.BlockSpec(memory_space=pltpu.HBM)
    anywhere = pl.BlockSpec(memory_space=pl.ANY)
    out = jax.ShapeDtypeStruct((chunk, BLOCK_TOK, width), jnp.bfloat16)
    dma = pltpu.SemaphoreType.DMA
    low = jnp.bfloat16
    grads = pl.pallas_call(
        functools.partial(main_kernel, H, C),
        out_shape=(out, out, out),
        in_specs=[hbm] * 6,
        out_specs=(anywhere,) * 3,
        scratch_shapes=[
            pltpu.VMEM((1,) + block_slot.shape, jnp.int32), pltpu.VMEM(neighbours.shape[::-1], jnp.int32),
            pltpu.VMEM((3, NBR, 128), jnp.int32), pltpu.SMEM((3, NBR, 128), jnp.int32), dma((4,)),
            pltpu.VMEM((T, BLOCK_TOK, 128), low), pltpu.VMEM((T, BLOCK_TOK, 128), low),
            pltpu.VMEM((3 * T, BLOCK_TOK, 128), low), pltpu.VMEM((3 * T, BLOCK_TOK, 128), low),
            pltpu.VMEM((pairs + 1, BLOCK_TOK, 128), jnp.float32),
            pltpu.VMEM((pairs + 1, BLOCK_TOK, 128), jnp.float32),
            pltpu.VMEM((T, BLOCK_TOK, 128), low),
            pltpu.VMEM((2 * T, BLOCK_TOK, 128), low), pltpu.VMEM((2 * T, BLOCK_TOK, 128), low),
            pltpu.VMEM((2 * T, BLOCK_TOK, 128), low), pltpu.VMEM((2 * T, BLOCK_TOK, 128), low),
            pltpu.VMEM((T, BLOCK_TOK, 128), low), pltpu.VMEM((T, BLOCK_TOK, 128), low),
            pltpu.VMEM((2, NBR * BLOCK_TOK, 128), jnp.float32), pltpu.VMEM((T, NBR * BLOCK_TOK, 128), jnp.float32),
            pltpu.VMEM((2, NBR * BLOCK_TOK, 128), jnp.float32),
            *[pltpu.VMEM((n, 8, 128), jnp.float32) for n in (2, T, 2)],
            dma((4, H)), dma((4, H)), dma((2, H, 2)), dma((2, H, 2)), dma((H,)), dma((H,)),
            dma((2, H, 2)), dma((2, H, 2)), dma((2, H)), dma((2, H)),
        ],
        compiler_params=pltpu.CompilerParams(collective_id=0, has_side_effects=True, vmem_limit_bytes=24 * 2**20),
        name="attention",
    )(*(pltpu.with_memory_space_constraint(x, pltpu.HBM) for x in (block_slot[None], neighbours.T) + tuple(
        x.reshape(chunk, BLOCK_TOK, width) for x in (queries, key_states, value_states, grad_output))))
    grads = pl.pallas_call(
        copy_kernel,
        out_shape=(out, out, out),
        in_specs=[anywhere] * 3,
        out_specs=(anywhere,) * 3,
        scratch_shapes=[dma((3, chunk))],
        compiler_params=pltpu.CompilerParams(vmem_limit_bytes=4 * 2**20),
        name="results",
    )(*grads)
    return tuple(x.reshape(rows, width) for x in grads)


def solution(mesh):
    tokens = P(("band", "ctx", "head"), None)
    in_specs = (tokens, tokens, tokens, tokens, P("band"), P("band", None))
    return jax.shard_map(body, mesh=mesh, in_specs=in_specs, out_specs=(tokens, tokens, tokens), check_vma=False)
```

```python
import functools
import math

import jax
import jax.numpy as jnp
from jax import lax
from jax.experimental import pallas as pl
from jax.experimental.pallas import tpu as pltpu
from jax.sharding import PartitionSpec as P

HEAD_DIM = 64
BLOCK_TOK = 64
NBR = 8
TILE_BLOCKS = 8
MESH = pl.DeviceIdType.MESH
NT = (((1,), (1,)), ((), ()))
NN = (((1,), (0,)), ((), ()))
TN = (((0,), (0,)), ((), ()))


def at_step(step, H):
    return lax.rem(jnp.where(step % 2 == 1, (step + 1) // 2, H - step // 2), H)


def copy_kernel(*refs):
    half = len(refs) // 2
    parts = [(i, k) for i in range(half) for k in range(refs[i].shape[0])]
    copies = [pltpu.make_async_copy(refs[i].at[k], refs[half + i].at[k], refs[-1].at[i, k]) for i, k in parts]
    for copy in copies:
        copy.start()
    for copy in copies:
        copy.wait()


def main_kernel(heads, ctx_size, slot_in, nbr_in, q_in, k_in, v_in, g_in, dq_out, dk_out, dv_out,
                slot_ref, nbr_ref, table_vec, table, table_sem, ring_sem, ctx_sem,
                q_loc, g_loc, k_span, v_span, run_k, run_v, dq_stage, part_k, part_v, back_k, back_v, sum_k, sum_v,
                score_buf, weight_buf, mixed_buf, top_buf, total_buf, stat_buf,
                in_send, in_recv, fwd_send, fwd_recv, dq_send, dq_recv, ret_send, ret_recv, out_send, out_recv):
    H = heads
    h = lax.axis_index("head")
    c = lax.axis_index("ctx")
    per_chunk = q_in.shape[0]
    T = H * per_chunk
    per_ctx = T
    pairs = per_ctx * NBR
    scale = HEAD_DIM ** -0.5
    ctx_prev = lax.rem(c + ctx_size - 1, ctx_size)
    ctx_next = lax.rem(c + 1, ctx_size)
    ctx_peer = (ctx_prev, ctx_next)

    def peer(d):
        return lax.rem(h + d, H)

    def source(d):
        return lax.rem(h + H - d, H)

    def rows(base, chunk):
        return pl.ds(base + chunk * per_chunk, per_chunk)

    def cols(chunk):
        return pl.ds(pl.multiple_of(chunk * 128, 128), 128)

    slot_copy = pltpu.make_async_copy(slot_in, slot_ref, table_sem.at[2])
    nbr_copy = pltpu.make_async_copy(nbr_in, nbr_ref, table_sem.at[3])
    slot_copy.start()
    nbr_copy.start()
    barrier = pltpu.get_barrier_semaphore()
    for d in range(1, H):
        pl.semaphore_signal(barrier, inc=1, device_id={"head": peer(d)}, device_id_type=MESH)
    @pl.when(h == 0)
    def _():
        for p in ctx_peer:
            pl.semaphore_signal(barrier, inc=1, device_id={"ctx": p}, device_id_type=MESH)
        pl.semaphore_wait(barrier, H + 1)

    @pl.when(h != 0)
    def _():
        pl.semaphore_wait(barrier, H - 1)

    order = [0]
    for step in range(1, H):
        order.append(((step + 1) // 2 if step % 2 else H - step // 2) % H)

    incoming = ((k_in, k_span, T), (v_in, v_span, T), (q_in, q_loc, 0), (g_in, g_loc, 0))

    def in_copy(t, d):
        src, dst, base = incoming[t]
        return pltpu.make_async_remote_copy(
            src_ref=src.at[:, :, cols(peer(d))], dst_ref=dst.at[rows(base, h)],
            send_sem=in_send.at[t, d], recv_sem=in_recv.at[t, d],
            device_id={"head": peer(d)}, device_id_type=MESH)

    def in_own(t):
        src, dst, base = incoming[t]
        return pltpu.make_async_copy(src.at[:, :, cols(h)], dst.at[rows(base, h)], in_recv.at[t, 0])

    def in_wait(t, d):
        src, dst, base = incoming[t]
        pltpu.make_async_remote_copy(
            src_ref=src.at[:, :, cols(peer(d))], dst_ref=dst.at[rows(base, source(d))],
            send_sem=in_send.at[t, d], recv_sem=in_recv.at[t, d],
            device_id={"head": peer(d)}, device_id_type=MESH).wait_recv()

    for t in range(4):
        in_own(t).start()
        for d in order[1:]:
            in_copy(t, d).start()

    @pl.when(h == 0)
    def _():
        for way in range(2):
            pl.semaphore_signal(ring_sem.at[way], inc=1, device_id={"ctx": ctx_peer[way]}, device_id_type=MESH)
        for way in range(2):
            pl.semaphore_wait(ring_sem.at[way], 1)
        for d in range(1, H):
            pl.semaphore_signal(ctx_sem, inc=1, device_id={"head": peer(d)}, device_id_type=MESH)

    def fwd_copy(t, d, way):
        span = incoming[t][1]
        chunk = source(d)
        return pltpu.make_async_remote_copy(
            src_ref=span.at[rows(T, chunk)],
            dst_ref=span.at[rows(2 * T if way == 0 else 0, chunk)],
            send_sem=fwd_send.at[t, d, way], recv_sem=fwd_recv.at[t, d, way],
            device_id={"ctx": ctx_peer[way]}, device_id_type=MESH)

    slot_copy.wait()
    nbr_copy.wait()
    slots = slot_ref.shape[1]
    slot_row = slot_ref[...]
    nbr = nbr_ref[...]
    slot_lane = lax.broadcasted_iota(jnp.int32, (NBR, slots), 1)
    lane = lax.broadcasted_iota(jnp.int32, (NBR, 128), 1)
    own = lane * NBR + lax.broadcasted_iota(jnp.int32, (NBR, 128), 0)
    targets = jnp.zeros((NBR, 128), jnp.int32)
    for turn in range(per_ctx):
        s = source(order[turn // per_chunk]) * per_chunk + turn % per_chunk
        near = jnp.sum(jnp.where(slot_row == c * per_ctx + s, nbr, 0), axis=1, keepdims=True)
        slot = jnp.sum(jnp.where(slot_lane == near, slot_row, 0), axis=1, keepdims=True)
        target = jnp.zeros_like(slot)
        for region, owner in enumerate((ctx_prev, c, ctx_next)):
            local = slot - owner * per_ctx
            target = jnp.where((local >= 0) & (local < per_ctx), local + region * per_ctx, target)
        targets = jnp.where(lane == turn, target, targets)
    table_vec[0] = targets
    first_half = pltpu.make_async_copy(table_vec.at[pl.ds(0, 1)], table.at[pl.ds(0, 1)], table_sem.at[0])
    first_half.start()
    first_half.wait()

    def chain(turn, carry):
        before, last = carry
        for n in range(NBR):
            target = table[0, n, turn]
            pair = turn * NBR + n
            before = jnp.where((targets == target) & (own > pair), pair, before)
            last = jnp.where(lane == target, pair, last)
        return before, last

    nothing = jnp.full((NBR, 128), pairs, jnp.int32)
    before, last = lax.fori_loop(0, per_ctx, chain, (nothing, nothing))
    table_vec[1] = before
    table_vec[2] = last
    second_half = pltpu.make_async_copy(table_vec.at[pl.ds(1, 2)], table.at[pl.ds(1, 2)], table_sem.at[1])
    second_half.start()
    second_half.wait()

    run_k[pairs] = jnp.zeros(run_k.shape[1:], jnp.float32)
    run_v[pairs] = jnp.zeros(run_v.shape[1:], jnp.float32)

    @pl.when(h != 0)
    def _():
        pl.semaphore_wait(ctx_sem, 1)

    for t in range(2):
        for d in order:
            if d == 0:
                in_own(t).wait()
            else:
                in_wait(t, d)
            for way in range(2):
                fwd_copy(t, d, way).start()

    def fwd_wait(t, d, way):
        span = incoming[t][1]
        chunk = source(d)
        pltpu.make_async_remote_copy(
            src_ref=span.at[rows(T, chunk)],
            dst_ref=span.at[rows(2 * T if way == 0 else 0, chunk)],
            send_sem=fwd_send.at[t, d, way], recv_sem=fwd_recv.at[t, d, way],
            device_id={"ctx": ctx_peer[way]}, device_id_type=MESH).wait_recv()

    def span_wait(t):
        for d in order:
            for way in range(2):
                fwd_wait(t, d, way)

    span_wait(0)

    low = (lax.broadcasted_iota(jnp.int32, (1, 128), 1) < HEAD_DIM).astype(jnp.float32)
    low_mask = low.astype(jnp.bfloat16)
    high_mask = (1.0 - low).astype(jnp.bfloat16)
    low_lanes = lax.broadcasted_iota(jnp.int32, (BLOCK_TOK, 128), 1) < HEAD_DIM
    exp_scale = scale * math.log2(math.e)

    tile = TILE_BLOCKS * BLOCK_TOK
    tiles = NBR // TILE_BLOCKS

    def slot_at(turn):
        step = turn // per_chunk
        return source(at_step(step, H)) * per_chunk + turn % per_chunk

    def diagonal(x):
        return jnp.concatenate([x * low_mask, x * high_mask], axis=0)

    def listed(span, turn, r):
        return jnp.concatenate([span[table[0, r * TILE_BLOCKS + n, turn]] for n in range(TILE_BLOCKS)], axis=0)

    def fold(x):
        return x.reshape(tile // 8, 8, 128)

    class Scores:
        def __init__(self, turn, side):
            self.turn, self.side = turn, side
            self.wq = diagonal(q_loc[slot_at(turn)])
            self.top = None

        def tile(self, r):
            part = pl.ds(r * tile, tile)
            scores = lax.dot_general(listed(k_span, self.turn, r), self.wq, NT, preferred_element_type=jnp.float32)
            score_buf[self.side, part, :] = scores
            top = jnp.max(fold(scores), axis=0)
            self.top = top if self.top is None else jnp.maximum(self.top, top)

        def finish(self):
            top_buf[self.side] = self.top

    class Weights:
        def __init__(self, turn, side):
            self.turn, self.side = turn, side
            self.top = jnp.max(top_buf[side], axis=0, keepdims=True)
            self.total = None

        def tile(self, r):
            part = pl.ds(r * tile, tile)
            weights = jnp.exp2((score_buf[self.side, part, :] - self.top) * exp_scale)
            weight_buf[self.turn, part, :] = weights
            total = jnp.sum(fold(weights), axis=0)
            self.total = total if self.total is None else self.total + total

        def finish(self):
            total_buf[self.turn] = self.total

    class Mixed:
        def __init__(self, turn, side):
            self.turn, self.side = turn, side
            self.wg = diagonal(g_loc[slot_at(turn)])
            self.mixed = None

        def tile(self, r):
            part = pl.ds(r * tile, tile)
            grad = lax.dot_general(listed(v_span, self.turn, r), self.wg, NT, preferred_element_type=jnp.float32)
            mixed = weight_buf[self.turn, part, :] * grad
            mixed_buf[self.side, part, :] = mixed
            mixed = jnp.sum(fold(mixed), axis=0)
            self.mixed = mixed if self.mixed is None else self.mixed + mixed

        def finish(self):
            stat_buf[self.side] = self.mixed

    class Gradients:
        def __init__(self, turn, side):
            self.turn, self.side = turn, side
            self.slot = slot_at(turn)
            self.wq, self.wg = diagonal(q_loc[self.slot]), diagonal(g_loc[self.slot])
            self.inverse = 1.0 / jnp.sum(total_buf[turn], axis=0, keepdims=True)
            self.delta = jnp.sum(stat_buf[side], axis=0, keepdims=True) * self.inverse
            self.dq = None

        def tile(self, r):
            part = pl.ds(r * tile, tile)
            prob = weight_buf[self.turn, part, :] * self.inverse
            score_low = (mixed_buf[self.side, part, :] * self.inverse - prob * self.delta).astype(jnp.bfloat16)
            prob_low = prob.astype(jnp.bfloat16)
            dv = lax.dot_general(prob_low, self.wg, NN, preferred_element_type=jnp.float32)
            dk = lax.dot_general(score_low, self.wq, NN, preferred_element_type=jnp.float32)
            dq = lax.dot_general(score_low, listed(k_span, self.turn, r), TN, preferred_element_type=jnp.float32)
            self.dq = dq if self.dq is None else self.dq + dq
            for k in range(TILE_BLOCKS):
                n = r * TILE_BLOCKS + k
                pair = self.turn * NBR + n
                before = table[1, n, self.turn]
                here = slice(k * BLOCK_TOK, (k + 1) * BLOCK_TOK)
                run_k[pair] = dk[here] + run_k[before]
                run_v[pair] = dv[here] + run_v[before]

        def finish(self):
            dq = jnp.where(low_lanes, self.dq[:BLOCK_TOK], self.dq[BLOCK_TOK:]) * scale
            dq_stage[self.slot] = dq.astype(jnp.bfloat16)

    def together(*stages):
        for r in range(tiles):
            for stage in stages:
                stage.tile(r)
        for stage in stages:
            stage.finish()

    def dq_copy(d):
        chunk = source(d)
        return pltpu.make_async_remote_copy(
            src_ref=dq_stage.at[rows(0, chunk)], dst_ref=dq_out.at[:, :, cols(h)],
            send_sem=dq_send.at[d], recv_sem=dq_recv.at[d],
            device_id={"head": chunk}, device_id_type=MESH)

    def dq_own():
        return pltpu.make_async_copy(dq_stage.at[rows(0, h)], dq_out.at[:, :, cols(h)], dq_recv.at[0])

    turns = H * per_chunk
    in_own(2).wait()
    together(Scores(0, 0))
    together(Weights(0, 0), Scores(1, 1))

    def first_step(step, carry):
        in_wait(2, at_step(step, H))
        turn = step * per_chunk
        together(Weights(turn - 1, 1), Scores(turn, 0))
        together(Weights(turn, 0), Scores(turn + 1, 1))
        return carry

    lax.fori_loop(1, H, first_step, 0)
    together(Weights(turns - 1, 1))

    span_wait(1)
    in_own(3).wait()
    together(Mixed(0, 0))
    together(Gradients(0, 0), Mixed(1, 1))

    def second_step(step, carry):
        in_wait(3, at_step(step, H))

        @pl.when(step == 2)
        def _():
            dq_own().start()

        @pl.when(step > 2)
        def _():
            dq_copy(at_step(step - 2, H)).start()

        turn = step * per_chunk
        together(Gradients(turn - 1, 1), Mixed(turn, 0))
        together(Gradients(turn, 0), Mixed(turn + 1, 1))
        return carry

    lax.fori_loop(1, H, second_step, 0)
    if H == 2:
        dq_own().start()
    else:
        dq_copy(order[H - 2]).start()
    together(Gradients(turns - 1, 1))
    dq_copy(order[H - 1]).start()

    back_order = order[::-1]

    def ret_copy(d, way, which):
        chunk = peer(d)
        part = (part_k, part_v)[which]
        back = (back_k, back_v)[which]
        return pltpu.make_async_remote_copy(
            src_ref=part.at[rows(way * T, chunk)], dst_ref=back.at[rows(way * T, chunk)],
            send_sem=ret_send.at[which, d, way], recv_sem=ret_recv.at[which, d, way],
            device_id={"ctx": ctx_peer[way]}, device_id_type=MESH)

    for d in back_order:
        chunk = peer(d)
        for way in range(2):
            region = 0 if way == 0 else 2
            for k in range(per_chunk):
                block = chunk * per_chunk + k
                end = table[2, 0, region * per_ctx + block]
                part_k[way * T + block] = (run_k[end] * scale).astype(jnp.bfloat16)
                part_v[way * T + block] = run_v[end].astype(jnp.bfloat16)
        for way in range(2):
            for which in range(2):
                ret_copy(d, way, which).start()

    def out_copy(d, which):
        chunk = peer(d)
        return pltpu.make_async_remote_copy(
            src_ref=(sum_k, sum_v)[which].at[rows(0, chunk)], dst_ref=(dk_out, dv_out)[which].at[:, :, cols(h)],
            send_sem=out_send.at[which, d], recv_sem=out_recv.at[which, d],
            device_id={"head": chunk}, device_id_type=MESH)

    def out_own(which):
        return pltpu.make_async_copy(
            (sum_k, sum_v)[which].at[rows(0, h)], (dk_out, dv_out)[which].at[:, :, cols(h)], out_recv.at[which, 0])

    for d in back_order:
        chunk = peer(d)
        for way in range(2):
            for which in range(2):
                ret_copy(d, way, which).wait_recv()
        for k in range(per_chunk):
            block = chunk * per_chunk + k
            end = table[2, 0, per_ctx + block]
            sum_k[block] = (run_k[end] * scale + back_k[block].astype(jnp.float32)
                            + back_k[T + block].astype(jnp.float32)).astype(jnp.bfloat16)
            sum_v[block] = (run_v[end] + back_v[block].astype(jnp.float32)
                            + back_v[T + block].astype(jnp.float32)).astype(jnp.bfloat16)
        for which in range(2):
            if d == 0:
                out_own(which).start()
            else:
                out_copy(d, which).start()

    dq_own().wait()
    for which in range(2):
        out_own(which).wait()
    for d in order[1:]:
        for t in range(4):
            in_copy(t, d).wait_send()
        dq_copy(d).wait_send()
        pltpu.make_async_remote_copy(
            src_ref=dq_stage.at[rows(0, peer(d))], dst_ref=dq_out.at[:, :, cols(peer(d))],
            send_sem=dq_send.at[d], recv_sem=dq_recv.at[d],
            device_id={"head": peer(d)}, device_id_type=MESH).wait_recv()
        for which in range(2):
            out_copy(d, which).wait_send()
            pltpu.make_async_remote_copy(
                src_ref=(sum_k, sum_v)[which].at[rows(0, source(d))],
                dst_ref=(dk_out, dv_out)[which].at[:, :, cols(source(d))],
                send_sem=out_send.at[which, d], recv_sem=out_recv.at[which, d],
                device_id={"head": source(d)}, device_id_type=MESH).wait_recv()
    for d in order:
        for way in range(2):
            for which in range(2):
                fwd_copy(which, d, way).wait_send()
                ret_copy(d, way, which).wait_send()


def body(queries, key_states, value_states, grad_output, block_slot, neighbours):
    H = lax.axis_size("head")
    C = lax.axis_size("ctx")
    rows, width = queries.shape
    chunk = rows // BLOCK_TOK
    per_ctx = chunk * H
    pairs = per_ctx * NBR
    T = per_ctx
    hbm = pl.BlockSpec(memory_space=pltpu.HBM)
    anywhere = pl.BlockSpec(memory_space=pl.ANY)
    out = jax.ShapeDtypeStruct((chunk, BLOCK_TOK, width), jnp.bfloat16)
    dma = pltpu.SemaphoreType.DMA
    low = jnp.bfloat16
    grads = pl.pallas_call(
        functools.partial(main_kernel, H, C),
        out_shape=(out, out, out),
        in_specs=[hbm] * 6,
        out_specs=(anywhere,) * 3,
        scratch_shapes=[
            pltpu.VMEM((1,) + block_slot.shape, jnp.int32), pltpu.VMEM(neighbours.shape[::-1], jnp.int32),
            pltpu.VMEM((3, NBR, 128), jnp.int32), pltpu.SMEM((3, NBR, 128), jnp.int32), dma((4,)),
            pltpu.SemaphoreType.REGULAR((2,)), pltpu.SemaphoreType.REGULAR,
            pltpu.VMEM((T, BLOCK_TOK, 128), low), pltpu.VMEM((T, BLOCK_TOK, 128), low),
            pltpu.VMEM((3 * T, BLOCK_TOK, 128), low), pltpu.VMEM((3 * T, BLOCK_TOK, 128), low),
            pltpu.VMEM((pairs + 1, BLOCK_TOK, 128), jnp.float32),
            pltpu.VMEM((pairs + 1, BLOCK_TOK, 128), jnp.float32),
            pltpu.VMEM((T, BLOCK_TOK, 128), low),
            pltpu.VMEM((2 * T, BLOCK_TOK, 128), low), pltpu.VMEM((2 * T, BLOCK_TOK, 128), low),
            pltpu.VMEM((2 * T, BLOCK_TOK, 128), low), pltpu.VMEM((2 * T, BLOCK_TOK, 128), low),
            pltpu.VMEM((T, BLOCK_TOK, 128), low), pltpu.VMEM((T, BLOCK_TOK, 128), low),
            pltpu.VMEM((2, NBR * BLOCK_TOK, 128), jnp.float32), pltpu.VMEM((T, NBR * BLOCK_TOK, 128), jnp.float32),
            pltpu.VMEM((2, NBR * BLOCK_TOK, 128), jnp.float32),
            *[pltpu.VMEM((n, 8, 128), jnp.float32) for n in (2, T, 2)],
            dma((4, H)), dma((4, H)), dma((2, H, 2)), dma((2, H, 2)), dma((H,)), dma((H,)),
            dma((2, H, 2)), dma((2, H, 2)), dma((2, H)), dma((2, H)),
        ],
        compiler_params=pltpu.CompilerParams(collective_id=0, has_side_effects=True, vmem_limit_bytes=24 * 2**20),
        name="attention",
    )(*(pltpu.with_memory_space_constraint(x, pltpu.HBM) for x in (block_slot[None], neighbours.T) + tuple(
        x.reshape(chunk, BLOCK_TOK, width) for x in (queries, key_states, value_states, grad_output))))
    grads = pl.pallas_call(
        copy_kernel,
        out_shape=(out, out, out),
        in_specs=[anywhere] * 3,
        out_specs=(anywhere,) * 3,
        scratch_shapes=[dma((3, chunk))],
        compiler_params=pltpu.CompilerParams(vmem_limit_bytes=4 * 2**20),
        name="results",
    )(*grads)
    return tuple(x.reshape(rows, width) for x in grads)


def solution(mesh):
    tokens = P(("band", "ctx", "head"), None)
    in_specs = (tokens, tokens, tokens, tokens, P("band"), P("band", None))
    return jax.shard_map(body, mesh=mesh, in_specs=in_specs, out_specs=(tokens, tokens, tokens), check_vma=False)
```

```python
import functools
import math

import jax
import jax.numpy as jnp
from jax import lax
from jax.experimental import pallas as pl
from jax.experimental.pallas import tpu as pltpu
from jax.sharding import PartitionSpec as P

HEAD_DIM = 64
BLOCK_TOK = 64
NBR = 8
TILE_BLOCKS = 8
MESH = pl.DeviceIdType.MESH
NT = (((1,), (1,)), ((), ()))
NN = (((1,), (0,)), ((), ()))
TN = (((0,), (0,)), ((), ()))


def at_step(step, H):
    return lax.rem(jnp.where(step % 2 == 1, (step + 1) // 2, H - step // 2), H)


def copy_kernel(*refs):
    half = len(refs) // 2
    parts = [(i, k) for i in range(half) for k in range(refs[i].shape[0])]
    copies = [pltpu.make_async_copy(refs[i].at[k], refs[half + i].at[k], refs[-1].at[i, k]) for i, k in parts]
    for copy in copies:
        copy.start()
    for copy in copies:
        copy.wait()


def main_kernel(heads, ctx_size, slot_in, nbr_in, q_in, k_in, v_in, g_in, dq_out, dk_out, dv_out,
                slot_ref, nbr_ref, table_vec, table, table_sem, ring_sem, ctx_sem,
                q_loc, g_loc, k_span, v_span, run_k, run_v, dq_stage, part_k, part_v, back_k, back_v, sum_k, sum_v,
                score_buf, weight_buf, mixed_buf, top_buf, total_buf, stat_buf,
                in_send, in_recv, fwd_send, fwd_recv, dq_send, dq_recv, ret_send, ret_recv, out_send, out_recv):
    H = heads
    h = lax.axis_index("head")
    c = lax.axis_index("ctx")
    per_chunk = q_in.shape[0]
    T = H * per_chunk
    per_ctx = T
    pairs = per_ctx * NBR
    scale = HEAD_DIM ** -0.5
    ctx_prev = lax.rem(c + ctx_size - 1, ctx_size)
    ctx_next = lax.rem(c + 1, ctx_size)
    ctx_peer = (ctx_prev, ctx_next)

    def peer(d):
        return lax.rem(h + d, H)

    def source(d):
        return lax.rem(h + H - d, H)

    def rows(base, chunk):
        return pl.ds(base + chunk * per_chunk, per_chunk)

    def cols(chunk):
        return pl.ds(pl.multiple_of(chunk * 128, 128), 128)

    slot_copy = pltpu.make_async_copy(slot_in, slot_ref, table_sem.at[2])
    nbr_copy = pltpu.make_async_copy(nbr_in, nbr_ref, table_sem.at[3])
    slot_copy.start()
    nbr_copy.start()
    barrier = pltpu.get_barrier_semaphore()
    for d in range(1, H):
        pl.semaphore_signal(barrier, inc=1, device_id={"head": peer(d)}, device_id_type=MESH)
    @pl.when(h == 0)
    def _():
        for p in ctx_peer:
            pl.semaphore_signal(barrier, inc=1, device_id={"ctx": p}, device_id_type=MESH)
        pl.semaphore_wait(barrier, H + 1)

    @pl.when(h != 0)
    def _():
        pl.semaphore_wait(barrier, H - 1)

    order = [0]
    for step in range(1, H):
        order.append(((step + 1) // 2 if step % 2 else H - step // 2) % H)

    incoming = ((k_in, k_span, T), (v_in, v_span, T), (q_in, q_loc, 0), (g_in, g_loc, 0))

    def in_copy(t, d):
        src, dst, base = incoming[t]
        return pltpu.make_async_remote_copy(
            src_ref=src.at[:, :, cols(peer(d))], dst_ref=dst.at[rows(base, h)],
            send_sem=in_send.at[t, d], recv_sem=in_recv.at[t, d],
            device_id={"head": peer(d)}, device_id_type=MESH)

    def in_own(t):
        src, dst, base = incoming[t]
        return pltpu.make_async_copy(src.at[:, :, cols(h)], dst.at[rows(base, h)], in_recv.at[t, 0])

    def in_wait(t, d):
        src, dst, base = incoming[t]
        pltpu.make_async_remote_copy(
            src_ref=src.at[:, :, cols(peer(d))], dst_ref=dst.at[rows(base, source(d))],
            send_sem=in_send.at[t, d], recv_sem=in_recv.at[t, d],
            device_id={"head": peer(d)}, device_id_type=MESH).wait_recv()

    for t in range(4):
        in_own(t).start()
        for d in order[1:]:
            in_copy(t, d).start()

    @pl.when(h == 0)
    def _():
        for way in range(2):
            pl.semaphore_signal(ring_sem.at[way], inc=1, device_id={"ctx": ctx_peer[way]}, device_id_type=MESH)
        for way in range(2):
            pl.semaphore_wait(ring_sem.at[way], 1)
        for d in range(1, H):
            pl.semaphore_signal(ctx_sem, inc=1, device_id={"head": peer(d)}, device_id_type=MESH)

    def fwd_copy(t, d, way):
        span = incoming[t][1]
        chunk = source(d)
        return pltpu.make_async_remote_copy(
            src_ref=span.at[rows(T, chunk)],
            dst_ref=span.at[rows(2 * T if way == 0 else 0, chunk)],
            send_sem=fwd_send.at[t, d, way], recv_sem=fwd_recv.at[t, d, way],
            device_id={"ctx": ctx_peer[way]}, device_id_type=MESH)

    slot_copy.wait()
    nbr_copy.wait()
    slots = slot_ref.shape[1]
    slot_row = slot_ref[...]
    nbr = nbr_ref[...]
    slot_lane = lax.broadcasted_iota(jnp.int32, (NBR, slots), 1)
    lane = lax.broadcasted_iota(jnp.int32, (NBR, 128), 1)
    own = lane * NBR + lax.broadcasted_iota(jnp.int32, (NBR, 128), 0)
    targets = jnp.zeros((NBR, 128), jnp.int32)
    for turn in range(per_ctx):
        s = source(order[turn // per_chunk]) * per_chunk + turn % per_chunk
        near = jnp.sum(jnp.where(slot_row == c * per_ctx + s, nbr, 0), axis=1, keepdims=True)
        slot = jnp.sum(jnp.where(slot_lane == near, slot_row, 0), axis=1, keepdims=True)
        target = jnp.zeros_like(slot)
        for region, owner in enumerate((ctx_prev, c, ctx_next)):
            local = slot - owner * per_ctx
            target = jnp.where((local >= 0) & (local < per_ctx), local + region * per_ctx, target)
        targets = jnp.where(lane == turn, target, targets)
    table_vec[0] = targets
    first_half = pltpu.make_async_copy(table_vec.at[pl.ds(0, 1)], table.at[pl.ds(0, 1)], table_sem.at[0])
    first_half.start()
    first_half.wait()

    def chain(turn, carry):
        before, last = carry
        for n in range(NBR):
            target = table[0, n, turn]
            pair = turn * NBR + n
            before = jnp.where((targets == target) & (own > pair), pair, before)
            last = jnp.where(lane == target, pair, last)
        return before, last

    nothing = jnp.full((NBR, 128), pairs, jnp.int32)
    before, last = lax.fori_loop(0, per_ctx, chain, (nothing, nothing))
    table_vec[1] = before
    table_vec[2] = last
    second_half = pltpu.make_async_copy(table_vec.at[pl.ds(1, 2)], table.at[pl.ds(1, 2)], table_sem.at[1])
    second_half.start()
    second_half.wait()

    run_k[pairs] = jnp.zeros(run_k.shape[1:], jnp.float32)
    run_v[pairs] = jnp.zeros(run_v.shape[1:], jnp.float32)

    @pl.when(h != 0)
    def _():
        pl.semaphore_wait(ctx_sem, 1)

    for t in range(2):
        for d in order:
            if d == 0:
                in_own(t).wait()
            else:
                in_wait(t, d)
            for way in range(2):
                fwd_copy(t, d, way).start()

    def fwd_wait(t, d, way):
        span = incoming[t][1]
        chunk = source(d)
        pltpu.make_async_remote_copy(
            src_ref=span.at[rows(T, chunk)],
            dst_ref=span.at[rows(2 * T if way == 0 else 0, chunk)],
            send_sem=fwd_send.at[t, d, way], recv_sem=fwd_recv.at[t, d, way],
            device_id={"ctx": ctx_peer[way]}, device_id_type=MESH).wait_recv()

    def span_wait(t):
        for d in order:
            for way in range(2):
                fwd_wait(t, d, way)

    span_wait(0)

    low = (lax.broadcasted_iota(jnp.int32, (1, 128), 1) < HEAD_DIM).astype(jnp.float32)
    low_mask = low.astype(jnp.bfloat16)
    high_mask = (1.0 - low).astype(jnp.bfloat16)
    low_lanes = lax.broadcasted_iota(jnp.int32, (BLOCK_TOK, 128), 1) < HEAD_DIM
    exp_scale = scale * math.log2(math.e)

    tile = TILE_BLOCKS * BLOCK_TOK
    tiles = NBR // TILE_BLOCKS

    def slot_at(turn):
        step = turn // per_chunk
        return source(at_step(step, H)) * per_chunk + turn % per_chunk

    def diagonal(x):
        return jnp.concatenate([x * low_mask, x * high_mask], axis=0)

    def listed(span, turn, r):
        return jnp.concatenate([span[table[0, r * TILE_BLOCKS + n, turn]] for n in range(TILE_BLOCKS)], axis=0)

    def fold(x):
        return x.reshape(tile // 8, 8, 128)

    class Scores:
        def __init__(self, turn, side):
            self.turn, self.side = turn, side
            self.wq = diagonal(q_loc[slot_at(turn)])
            self.top = None

        def tile(self, r):
            part = pl.ds(r * tile, tile)
            scores = lax.dot_general(listed(k_span, self.turn, r), self.wq, NT, preferred_element_type=jnp.float32)
            score_buf[self.side, part, :] = scores
            top = jnp.max(fold(scores), axis=0)
            self.top = top if self.top is None else jnp.maximum(self.top, top)

        def finish(self):
            top_buf[self.side] = self.top

    class Weights:
        def __init__(self, turn, side):
            self.turn, self.side = turn, side
            self.top = jnp.max(top_buf[side], axis=0, keepdims=True)
            self.total = None

        def tile(self, r):
            part = pl.ds(r * tile, tile)
            weights = jnp.exp2((score_buf[self.side, part, :] - self.top) * exp_scale)
            weight_buf[self.turn, part, :] = weights
            total = jnp.sum(fold(weights), axis=0)
            self.total = total if self.total is None else self.total + total

        def finish(self):
            total_buf[self.turn] = self.total

    class Mixed:
        def __init__(self, turn, side):
            self.turn, self.side = turn, side
            self.wg = diagonal(g_loc[slot_at(turn)])
            self.mixed = None

        def tile(self, r):
            part = pl.ds(r * tile, tile)
            grad = lax.dot_general(listed(v_span, self.turn, r), self.wg, NT, preferred_element_type=jnp.float32)
            mixed = weight_buf[self.turn, part, :] * grad
            mixed_buf[self.side, part, :] = mixed
            mixed = jnp.sum(fold(mixed), axis=0)
            self.mixed = mixed if self.mixed is None else self.mixed + mixed

        def finish(self):
            stat_buf[self.side] = self.mixed

    class Gradients:
        def __init__(self, turn, side):
            self.turn, self.side = turn, side
            self.slot = slot_at(turn)
            self.wq, self.wg = diagonal(q_loc[self.slot]), diagonal(g_loc[self.slot])
            self.inverse = 1.0 / jnp.sum(total_buf[turn], axis=0, keepdims=True)
            self.delta = jnp.sum(stat_buf[side], axis=0, keepdims=True) * self.inverse
            self.dq = None

        def tile(self, r):
            part = pl.ds(r * tile, tile)
            prob = weight_buf[self.turn, part, :] * self.inverse
            score_low = (mixed_buf[self.side, part, :] * self.inverse - prob * self.delta).astype(jnp.bfloat16)
            prob_low = prob.astype(jnp.bfloat16)
            dv = lax.dot_general(prob_low, self.wg, NN, preferred_element_type=jnp.float32)
            dk = lax.dot_general(score_low, self.wq, NN, preferred_element_type=jnp.float32)
            dq = lax.dot_general(score_low, listed(k_span, self.turn, r), TN, preferred_element_type=jnp.float32)
            self.dq = dq if self.dq is None else self.dq + dq
            for k in range(TILE_BLOCKS):
                n = r * TILE_BLOCKS + k
                pair = self.turn * NBR + n
                before = table[1, n, self.turn]
                here = slice(k * BLOCK_TOK, (k + 1) * BLOCK_TOK)
                run_k[pair] = dk[here] + run_k[before]
                run_v[pair] = dv[here] + run_v[before]

        def finish(self):
            dq = jnp.where(low_lanes, self.dq[:BLOCK_TOK], self.dq[BLOCK_TOK:]) * scale
            dq_stage[self.slot] = dq.astype(jnp.bfloat16)

    def together(*stages):
        for r in range(tiles):
            for stage in stages:
                stage.tile(r)
        for stage in stages:
            stage.finish()

    def dq_copy(d):
        chunk = source(d)
        return pltpu.make_async_remote_copy(
            src_ref=dq_stage.at[rows(0, chunk)], dst_ref=dq_out.at[:, :, cols(h)],
            send_sem=dq_send.at[d], recv_sem=dq_recv.at[d],
            device_id={"head": chunk}, device_id_type=MESH)

    def dq_own():
        return pltpu.make_async_copy(dq_stage.at[rows(0, h)], dq_out.at[:, :, cols(h)], dq_recv.at[0])

    turns = H * per_chunk
    in_own(2).wait()
    together(*[Scores(k, k) for k in range(per_chunk)])

    def first_step(step, carry):
        in_wait(2, at_step(step, H))
        turn = step * per_chunk
        together(*[Weights(turn - per_chunk + k, k) for k in range(per_chunk)],
                 *[Scores(turn + k, k) for k in range(per_chunk)])
        return carry

    lax.fori_loop(1, H, first_step, 0)
    together(*[Weights(turns - per_chunk + k, k) for k in range(per_chunk)])

    span_wait(1)
    in_own(3).wait()
    together(*[Mixed(k, k) for k in range(per_chunk)])

    def second_step(step, carry):
        in_wait(3, at_step(step, H))

        @pl.when(step == 2)
        def _():
            dq_own().start()

        @pl.when(step > 2)
        def _():
            dq_copy(at_step(step - 2, H)).start()

        turn = step * per_chunk
        together(*[Gradients(turn - per_chunk + k, k) for k in range(per_chunk)],
                 *[Mixed(turn + k, k) for k in range(per_chunk)])
        return carry

    lax.fori_loop(1, H, second_step, 0)
    if H == 2:
        dq_own().start()
    else:
        dq_copy(order[H - 2]).start()
    together(*[Gradients(turns - per_chunk + k, k) for k in range(per_chunk)])
    dq_copy(order[H - 1]).start()

    back_order = order[::-1]

    def ret_copy(d, way, which):
        chunk = peer(d)
        part = (part_k, part_v)[which]
        back = (back_k, back_v)[which]
        return pltpu.make_async_remote_copy(
            src_ref=part.at[rows(way * T, chunk)], dst_ref=back.at[rows(way * T, chunk)],
            send_sem=ret_send.at[which, d, way], recv_sem=ret_recv.at[which, d, way],
            device_id={"ctx": ctx_peer[way]}, device_id_type=MESH)

    for d in back_order:
        chunk = peer(d)
        for way in range(2):
            region = 0 if way == 0 else 2
            for k in range(per_chunk):
                block = chunk * per_chunk + k
                end = table[2, 0, region * per_ctx + block]
                part_k[way * T + block] = (run_k[end] * scale).astype(jnp.bfloat16)
                part_v[way * T + block] = run_v[end].astype(jnp.bfloat16)
        for way in range(2):
            for which in range(2):
                ret_copy(d, way, which).start()

    def out_copy(d, which):
        chunk = peer(d)
        return pltpu.make_async_remote_copy(
            src_ref=(sum_k, sum_v)[which].at[rows(0, chunk)], dst_ref=(dk_out, dv_out)[which].at[:, :, cols(h)],
            send_sem=out_send.at[which, d], recv_sem=out_recv.at[which, d],
            device_id={"head": chunk}, device_id_type=MESH)

    def out_own(which):
        return pltpu.make_async_copy(
            (sum_k, sum_v)[which].at[rows(0, h)], (dk_out, dv_out)[which].at[:, :, cols(h)], out_recv.at[which, 0])

    for d in back_order:
        chunk = peer(d)
        for way in range(2):
            for which in range(2):
                ret_copy(d, way, which).wait_recv()
        for k in range(per_chunk):
            block = chunk * per_chunk + k
            end = table[2, 0, per_ctx + block]
            sum_k[block] = (run_k[end] * scale + back_k[block].astype(jnp.float32)
                            + back_k[T + block].astype(jnp.float32)).astype(jnp.bfloat16)
            sum_v[block] = (run_v[end] + back_v[block].astype(jnp.float32)
                            + back_v[T + block].astype(jnp.float32)).astype(jnp.bfloat16)
        for which in range(2):
            if d == 0:
                out_own(which).start()
            else:
                out_copy(d, which).start()

    dq_own().wait()
    for which in range(2):
        out_own(which).wait()
    for d in order[1:]:
        for t in range(4):
            in_copy(t, d).wait_send()
        dq_copy(d).wait_send()
        pltpu.make_async_remote_copy(
            src_ref=dq_stage.at[rows(0, peer(d))], dst_ref=dq_out.at[:, :, cols(peer(d))],
            send_sem=dq_send.at[d], recv_sem=dq_recv.at[d],
            device_id={"head": peer(d)}, device_id_type=MESH).wait_recv()
        for which in range(2):
            out_copy(d, which).wait_send()
            pltpu.make_async_remote_copy(
                src_ref=(sum_k, sum_v)[which].at[rows(0, source(d))],
                dst_ref=(dk_out, dv_out)[which].at[:, :, cols(source(d))],
                send_sem=out_send.at[which, d], recv_sem=out_recv.at[which, d],
                device_id={"head": source(d)}, device_id_type=MESH).wait_recv()
    for d in order:
        for way in range(2):
            for which in range(2):
                fwd_copy(which, d, way).wait_send()
                ret_copy(d, way, which).wait_send()


def body(queries, key_states, value_states, grad_output, block_slot, neighbours):
    H = lax.axis_size("head")
    C = lax.axis_size("ctx")
    rows, width = queries.shape
    chunk = rows // BLOCK_TOK
    per_ctx = chunk * H
    pairs = per_ctx * NBR
    T = per_ctx
    hbm = pl.BlockSpec(memory_space=pltpu.HBM)
    anywhere = pl.BlockSpec(memory_space=pl.ANY)
    out = jax.ShapeDtypeStruct((chunk, BLOCK_TOK, width), jnp.bfloat16)
    dma = pltpu.SemaphoreType.DMA
    low = jnp.bfloat16
    grads = pl.pallas_call(
        functools.partial(main_kernel, H, C),
        out_shape=(out, out, out),
        in_specs=[hbm] * 6,
        out_specs=(anywhere,) * 3,
        scratch_shapes=[
            pltpu.VMEM((1,) + block_slot.shape, jnp.int32), pltpu.VMEM(neighbours.shape[::-1], jnp.int32),
            pltpu.VMEM((3, NBR, 128), jnp.int32), pltpu.SMEM((3, NBR, 128), jnp.int32), dma((4,)),
            pltpu.SemaphoreType.REGULAR((2,)), pltpu.SemaphoreType.REGULAR,
            pltpu.VMEM((T, BLOCK_TOK, 128), low), pltpu.VMEM((T, BLOCK_TOK, 128), low),
            pltpu.VMEM((3 * T, BLOCK_TOK, 128), low), pltpu.VMEM((3 * T, BLOCK_TOK, 128), low),
            pltpu.VMEM((pairs + 1, BLOCK_TOK, 128), jnp.float32),
            pltpu.VMEM((pairs + 1, BLOCK_TOK, 128), jnp.float32),
            pltpu.VMEM((T, BLOCK_TOK, 128), low),
            pltpu.VMEM((2 * T, BLOCK_TOK, 128), low), pltpu.VMEM((2 * T, BLOCK_TOK, 128), low),
            pltpu.VMEM((2 * T, BLOCK_TOK, 128), low), pltpu.VMEM((2 * T, BLOCK_TOK, 128), low),
            pltpu.VMEM((T, BLOCK_TOK, 128), low), pltpu.VMEM((T, BLOCK_TOK, 128), low),
            pltpu.VMEM((chunk, NBR * BLOCK_TOK, 128), jnp.float32), pltpu.VMEM((T, NBR * BLOCK_TOK, 128), jnp.float32),
            pltpu.VMEM((chunk, NBR * BLOCK_TOK, 128), jnp.float32),
            *[pltpu.VMEM((n, 8, 128), jnp.float32) for n in (chunk, T, chunk)],
            dma((4, H)), dma((4, H)), dma((2, H, 2)), dma((2, H, 2)), dma((H,)), dma((H,)),
            dma((2, H, 2)), dma((2, H, 2)), dma((2, H)), dma((2, H)),
        ],
        compiler_params=pltpu.CompilerParams(collective_id=0, has_side_effects=True, vmem_limit_bytes=24 * 2**20),
        name="attention",
    )(*(pltpu.with_memory_space_constraint(x, pltpu.HBM) for x in (block_slot[None], neighbours.T) + tuple(
        x.reshape(chunk, BLOCK_TOK, width) for x in (queries, key_states, value_states, grad_output))))
    grads = pl.pallas_call(
        copy_kernel,
        out_shape=(out, out, out),
        in_specs=[anywhere] * 3,
        out_specs=(anywhere,) * 3,
        scratch_shapes=[dma((3, chunk))],
        compiler_params=pltpu.CompilerParams(vmem_limit_bytes=4 * 2**20),
        name="results",
    )(*grads)
    return tuple(x.reshape(rows, width) for x in grads)


def solution(mesh):
    tokens = P(("band", "ctx", "head"), None)
    in_specs = (tokens, tokens, tokens, tokens, P("band"), P("band", None))
    return jax.shard_map(body, mesh=mesh, in_specs=in_specs, out_specs=(tokens, tokens, tokens), check_vma=False)
```

```python
import functools
import math

import jax
import jax.numpy as jnp
from jax import lax
from jax.experimental import pallas as pl
from jax.experimental.pallas import tpu as pltpu
from jax.sharding import PartitionSpec as P

HEAD_DIM = 64
BLOCK_TOK = 64
NBR = 8
TILE_BLOCKS = 8
MESH = pl.DeviceIdType.MESH
NT = (((1,), (1,)), ((), ()))
NN = (((1,), (0,)), ((), ()))
TN = (((0,), (0,)), ((), ()))


def at_step(step, H):
    return lax.rem(jnp.where(step % 2 == 1, (step + 1) // 2, H - step // 2), H)


def copy_kernel(*refs):
    half = len(refs) // 2
    parts = [(i, k) for i in range(half) for k in range(refs[i].shape[0])]
    copies = [pltpu.make_async_copy(refs[i].at[k], refs[half + i].at[k], refs[-1].at[i, k]) for i, k in parts]
    for copy in copies:
        copy.start()
    for copy in copies:
        copy.wait()


def main_kernel(heads, ctx_size, slot_in, nbr_in, q_in, k_in, v_in, g_in, dq_out, dk_out, dv_out,
                slot_ref, nbr_ref, table_vec, table, table_sem, ring_sem, ctx_sem,
                q_loc, g_loc, k_span, v_span, run_k, run_v, dq_stage, part_k, part_v, back_k, back_v, sum_k, sum_v,
                score_buf, weight_buf, mixed_buf, top_buf, total_buf, stat_buf,
                in_send, in_recv, fwd_send, fwd_recv, dq_send, dq_recv, ret_send, ret_recv, out_send, out_recv):
    H = heads
    h = lax.axis_index("head")
    c = lax.axis_index("ctx")
    per_chunk = q_in.shape[0]
    T = H * per_chunk
    per_ctx = T
    pairs = per_ctx * NBR
    scale = HEAD_DIM ** -0.5
    ctx_prev = lax.rem(c + ctx_size - 1, ctx_size)
    ctx_next = lax.rem(c + 1, ctx_size)
    ctx_peer = (ctx_prev, ctx_next)

    def peer(d):
        return lax.rem(h + d, H)

    def source(d):
        return lax.rem(h + H - d, H)

    def rows(base, chunk):
        return pl.ds(base + chunk * per_chunk, per_chunk)

    def cols(chunk):
        return pl.ds(pl.multiple_of(chunk * 128, 128), 128)

    slot_copy = pltpu.make_async_copy(slot_in, slot_ref, table_sem.at[2])
    nbr_copy = pltpu.make_async_copy(nbr_in, nbr_ref, table_sem.at[3])
    slot_copy.start()
    nbr_copy.start()
    barrier = pltpu.get_barrier_semaphore()
    for d in range(1, H):
        pl.semaphore_signal(barrier, inc=1, device_id={"head": peer(d)}, device_id_type=MESH)
    @pl.when(h == 0)
    def _():
        for p in ctx_peer:
            pl.semaphore_signal(barrier, inc=1, device_id={"ctx": p}, device_id_type=MESH)
        pl.semaphore_wait(barrier, H + 1)

    @pl.when(h != 0)
    def _():
        pl.semaphore_wait(barrier, H - 1)

    order = [0]
    for step in range(1, H):
        order.append(((step + 1) // 2 if step % 2 else H - step // 2) % H)

    incoming = ((k_in, k_span, T), (v_in, v_span, T), (q_in, q_loc, 0), (g_in, g_loc, 0))

    def in_copy(t, d):
        src, dst, base = incoming[t]
        return pltpu.make_async_remote_copy(
            src_ref=src.at[:, :, cols(peer(d))], dst_ref=dst.at[rows(base, h)],
            send_sem=in_send.at[t, d], recv_sem=in_recv.at[t, d],
            device_id={"head": peer(d)}, device_id_type=MESH)

    def in_own(t):
        src, dst, base = incoming[t]
        return pltpu.make_async_copy(src.at[:, :, cols(h)], dst.at[rows(base, h)], in_recv.at[t, 0])

    def in_wait(t, d):
        src, dst, base = incoming[t]
        pltpu.make_async_remote_copy(
            src_ref=src.at[:, :, cols(peer(d))], dst_ref=dst.at[rows(base, source(d))],
            send_sem=in_send.at[t, d], recv_sem=in_recv.at[t, d],
            device_id={"head": peer(d)}, device_id_type=MESH).wait_recv()

    far_first = order[:0:-1]
    for t in range(4):
        in_own(t).start()
        for d in far_first if t < 2 else order[1:]:
            in_copy(t, d).start()

    @pl.when(h == 0)
    def _():
        for way in range(2):
            pl.semaphore_signal(ring_sem.at[way], inc=1, device_id={"ctx": ctx_peer[way]}, device_id_type=MESH)
        for way in range(2):
            pl.semaphore_wait(ring_sem.at[way], 1)
        for d in range(1, H):
            pl.semaphore_signal(ctx_sem, inc=1, device_id={"head": peer(d)}, device_id_type=MESH)

    def fwd_copy(t, d, way):
        span = incoming[t][1]
        chunk = source(d)
        return pltpu.make_async_remote_copy(
            src_ref=span.at[rows(T, chunk)],
            dst_ref=span.at[rows(2 * T if way == 0 else 0, chunk)],
            send_sem=fwd_send.at[t, d, way], recv_sem=fwd_recv.at[t, d, way],
            device_id={"ctx": ctx_peer[way]}, device_id_type=MESH)

    slot_copy.wait()
    nbr_copy.wait()
    slots = slot_ref.shape[1]
    slot_row = slot_ref[...]
    nbr = nbr_ref[...]
    slot_lane = lax.broadcasted_iota(jnp.int32, (NBR, slots), 1)
    lane = lax.broadcasted_iota(jnp.int32, (NBR, 128), 1)
    own = lane * NBR + lax.broadcasted_iota(jnp.int32, (NBR, 128), 0)
    targets = jnp.zeros((NBR, 128), jnp.int32)
    for turn in range(per_ctx):
        s = source(order[turn // per_chunk]) * per_chunk + turn % per_chunk
        near = jnp.sum(jnp.where(slot_row == c * per_ctx + s, nbr, 0), axis=1, keepdims=True)
        slot = jnp.sum(jnp.where(slot_lane == near, slot_row, 0), axis=1, keepdims=True)
        target = jnp.zeros_like(slot)
        for region, owner in enumerate((ctx_prev, c, ctx_next)):
            local = slot - owner * per_ctx
            target = jnp.where((local >= 0) & (local < per_ctx), local + region * per_ctx, target)
        targets = jnp.where(lane == turn, target, targets)
    table_vec[0] = targets
    first_half = pltpu.make_async_copy(table_vec.at[pl.ds(0, 1)], table.at[pl.ds(0, 1)], table_sem.at[0])
    first_half.start()
    first_half.wait()

    def chain(turn, carry):
        before, last = carry
        for n in range(NBR):
            target = table[0, n, turn]
            pair = turn * NBR + n
            before = jnp.where((targets == target) & (own > pair), pair, before)
            last = jnp.where(lane == target, pair, last)
        return before, last

    nothing = jnp.full((NBR, 128), pairs, jnp.int32)
    before, last = lax.fori_loop(0, per_ctx, chain, (nothing, nothing))
    table_vec[1] = before
    table_vec[2] = last
    second_half = pltpu.make_async_copy(table_vec.at[pl.ds(1, 2)], table.at[pl.ds(1, 2)], table_sem.at[1])
    second_half.start()
    second_half.wait()

    run_k[pairs] = jnp.zeros(run_k.shape[1:], jnp.float32)
    run_v[pairs] = jnp.zeros(run_v.shape[1:], jnp.float32)

    @pl.when(h != 0)
    def _():
        pl.semaphore_wait(ctx_sem, 1)

    for t in range(2):
        for d in order[:1] + far_first:
            if d == 0:
                in_own(t).wait()
            else:
                in_wait(t, d)
            for way in range(2):
                fwd_copy(t, d, way).start()

    def fwd_wait(t, d, way):
        span = incoming[t][1]
        chunk = source(d)
        pltpu.make_async_remote_copy(
            src_ref=span.at[rows(T, chunk)],
            dst_ref=span.at[rows(2 * T if way == 0 else 0, chunk)],
            send_sem=fwd_send.at[t, d, way], recv_sem=fwd_recv.at[t, d, way],
            device_id={"ctx": ctx_peer[way]}, device_id_type=MESH).wait_recv()

    def span_wait(t):
        for d in order:
            for way in range(2):
                fwd_wait(t, d, way)

    span_wait(0)

    low = (lax.broadcasted_iota(jnp.int32, (1, 128), 1) < HEAD_DIM).astype(jnp.float32)
    low_mask = low.astype(jnp.bfloat16)
    high_mask = (1.0 - low).astype(jnp.bfloat16)
    low_lanes = lax.broadcasted_iota(jnp.int32, (BLOCK_TOK, 128), 1) < HEAD_DIM
    exp_scale = scale * math.log2(math.e)

    tile = TILE_BLOCKS * BLOCK_TOK
    tiles = NBR // TILE_BLOCKS

    def slot_at(turn):
        step = turn // per_chunk
        return source(at_step(step, H)) * per_chunk + turn % per_chunk

    def diagonal(x):
        return jnp.concatenate([x * low_mask, x * high_mask], axis=0)

    def listed(span, turn, r):
        return jnp.concatenate([span[table[0, r * TILE_BLOCKS + n, turn]] for n in range(TILE_BLOCKS)], axis=0)

    def fold(x):
        return x.reshape(tile // 8, 8, 128)

    class Scores:
        def __init__(self, turn, side):
            self.turn, self.side = turn, side
            self.wq = diagonal(q_loc[slot_at(turn)])
            self.top = None

        def tile(self, r):
            part = pl.ds(r * tile, tile)
            scores = lax.dot_general(listed(k_span, self.turn, r), self.wq, NT, preferred_element_type=jnp.float32)
            score_buf[self.side, part, :] = scores
            top = jnp.max(fold(scores), axis=0)
            self.top = top if self.top is None else jnp.maximum(self.top, top)

        def finish(self):
            top_buf[self.side] = self.top

    class Weights:
        def __init__(self, turn, side):
            self.turn, self.side = turn, side
            self.top = jnp.max(top_buf[side], axis=0, keepdims=True)
            self.total = None

        def tile(self, r):
            part = pl.ds(r * tile, tile)
            weights = jnp.exp2((score_buf[self.side, part, :] - self.top) * exp_scale)
            weight_buf[self.turn, part, :] = weights
            total = jnp.sum(fold(weights), axis=0)
            self.total = total if self.total is None else self.total + total

        def finish(self):
            total_buf[self.turn] = self.total

    class Mixed:
        def __init__(self, turn, side):
            self.turn, self.side = turn, side
            self.wg = diagonal(g_loc[slot_at(turn)])
            self.mixed = None

        def tile(self, r):
            part = pl.ds(r * tile, tile)
            grad = lax.dot_general(listed(v_span, self.turn, r), self.wg, NT, preferred_element_type=jnp.float32)
            mixed = weight_buf[self.turn, part, :] * grad
            mixed_buf[self.side, part, :] = mixed
            mixed = jnp.sum(fold(mixed), axis=0)
            self.mixed = mixed if self.mixed is None else self.mixed + mixed

        def finish(self):
            stat_buf[self.side] = self.mixed

    class Gradients:
        def __init__(self, turn, side):
            self.turn, self.side = turn, side
            self.slot = slot_at(turn)
            self.wq, self.wg = diagonal(q_loc[self.slot]), diagonal(g_loc[self.slot])
            self.inverse = 1.0 / jnp.sum(total_buf[turn], axis=0, keepdims=True)
            self.delta = jnp.sum(stat_buf[side], axis=0, keepdims=True) * self.inverse
            self.dq = None

        def tile(self, r):
            part = pl.ds(r * tile, tile)
            prob = weight_buf[self.turn, part, :] * self.inverse
            score_low = (mixed_buf[self.side, part, :] * self.inverse - prob * self.delta).astype(jnp.bfloat16)
            prob_low = prob.astype(jnp.bfloat16)
            dv = lax.dot_general(prob_low, self.wg, NN, preferred_element_type=jnp.float32)
            dk = lax.dot_general(score_low, self.wq, NN, preferred_element_type=jnp.float32)
            dq = lax.dot_general(score_low, listed(k_span, self.turn, r), TN, preferred_element_type=jnp.float32)
            self.dq = dq if self.dq is None else self.dq + dq
            for k in range(TILE_BLOCKS):
                n = r * TILE_BLOCKS + k
                pair = self.turn * NBR + n
                before = table[1, n, self.turn]
                here = slice(k * BLOCK_TOK, (k + 1) * BLOCK_TOK)
                run_k[pair] = dk[here] + run_k[before]
                run_v[pair] = dv[here] + run_v[before]

        def finish(self):
            dq = jnp.where(low_lanes, self.dq[:BLOCK_TOK], self.dq[BLOCK_TOK:]) * scale
            dq_stage[self.slot] = dq.astype(jnp.bfloat16)

    def together(*stages):
        for r in range(tiles):
            for stage in stages:
                stage.tile(r)
        for stage in stages:
            stage.finish()

    def dq_copy(d):
        chunk = source(d)
        return pltpu.make_async_remote_copy(
            src_ref=dq_stage.at[rows(0, chunk)], dst_ref=dq_out.at[:, :, cols(h)],
            send_sem=dq_send.at[d], recv_sem=dq_recv.at[d],
            device_id={"head": chunk}, device_id_type=MESH)

    def dq_own():
        return pltpu.make_async_copy(dq_stage.at[rows(0, h)], dq_out.at[:, :, cols(h)], dq_recv.at[0])

    turns = H * per_chunk
    in_own(2).wait()
    together(*[Scores(k, k) for k in range(per_chunk)])

    def first_step(step, carry):
        in_wait(2, at_step(step, H))
        turn = step * per_chunk
        together(*[Weights(turn - per_chunk + k, k) for k in range(per_chunk)],
                 *[Scores(turn + k, k) for k in range(per_chunk)])
        return carry

    lax.fori_loop(1, H, first_step, 0)
    together(*[Weights(turns - per_chunk + k, k) for k in range(per_chunk)])

    span_wait(1)
    in_own(3).wait()
    together(*[Mixed(k, k) for k in range(per_chunk)])

    def second_step(step, carry):
        in_wait(3, at_step(step, H))

        @pl.when(step == 2)
        def _():
            dq_own().start()

        @pl.when(step > 2)
        def _():
            dq_copy(at_step(step - 2, H)).start()

        turn = step * per_chunk
        together(*[Gradients(turn - per_chunk + k, k) for k in range(per_chunk)],
                 *[Mixed(turn + k, k) for k in range(per_chunk)])
        return carry

    lax.fori_loop(1, H, second_step, 0)
    if H == 2:
        dq_own().start()
    else:
        dq_copy(order[H - 2]).start()
    together(*[Gradients(turns - per_chunk + k, k) for k in range(per_chunk)])
    dq_copy(order[H - 1]).start()

    back_order = order[::-1]

    def ret_copy(d, way, which):
        chunk = peer(d)
        part = (part_k, part_v)[which]
        back = (back_k, back_v)[which]
        return pltpu.make_async_remote_copy(
            src_ref=part.at[rows(way * T, chunk)], dst_ref=back.at[rows(way * T, chunk)],
            send_sem=ret_send.at[which, d, way], recv_sem=ret_recv.at[which, d, way],
            device_id={"ctx": ctx_peer[way]}, device_id_type=MESH)

    for d in back_order:
        chunk = peer(d)
        for way in range(2):
            region = 0 if way == 0 else 2
            for k in range(per_chunk):
                block = chunk * per_chunk + k
                end = table[2, 0, region * per_ctx + block]
                part_k[way * T + block] = (run_k[end] * scale).astype(jnp.bfloat16)
                part_v[way * T + block] = run_v[end].astype(jnp.bfloat16)
        for way in range(2):
            for which in range(2):
                ret_copy(d, way, which).start()

    def out_copy(d, which):
        chunk = peer(d)
        return pltpu.make_async_remote_copy(
            src_ref=(sum_k, sum_v)[which].at[rows(0, chunk)], dst_ref=(dk_out, dv_out)[which].at[:, :, cols(h)],
            send_sem=out_send.at[which, d], recv_sem=out_recv.at[which, d],
            device_id={"head": chunk}, device_id_type=MESH)

    def out_own(which):
        return pltpu.make_async_copy(
            (sum_k, sum_v)[which].at[rows(0, h)], (dk_out, dv_out)[which].at[:, :, cols(h)], out_recv.at[which, 0])

    for d in back_order:
        chunk = peer(d)
        for way in range(2):
            for which in range(2):
                ret_copy(d, way, which).wait_recv()
        for k in range(per_chunk):
            block = chunk * per_chunk + k
            end = table[2, 0, per_ctx + block]
            sum_k[block] = (run_k[end] * scale + back_k[block].astype(jnp.float32)
                            + back_k[T + block].astype(jnp.float32)).astype(jnp.bfloat16)
            sum_v[block] = (run_v[end] + back_v[block].astype(jnp.float32)
                            + back_v[T + block].astype(jnp.float32)).astype(jnp.bfloat16)
        for which in range(2):
            if d == 0:
                out_own(which).start()
            else:
                out_copy(d, which).start()

    dq_own().wait()
    for which in range(2):
        out_own(which).wait()
    for d in order[1:]:
        for t in range(4):
            in_copy(t, d).wait_send()
        dq_copy(d).wait_send()
        pltpu.make_async_remote_copy(
            src_ref=dq_stage.at[rows(0, peer(d))], dst_ref=dq_out.at[:, :, cols(peer(d))],
            send_sem=dq_send.at[d], recv_sem=dq_recv.at[d],
            device_id={"head": peer(d)}, device_id_type=MESH).wait_recv()
        for which in range(2):
            out_copy(d, which).wait_send()
            pltpu.make_async_remote_copy(
                src_ref=(sum_k, sum_v)[which].at[rows(0, source(d))],
                dst_ref=(dk_out, dv_out)[which].at[:, :, cols(source(d))],
                send_sem=out_send.at[which, d], recv_sem=out_recv.at[which, d],
                device_id={"head": source(d)}, device_id_type=MESH).wait_recv()
    for d in order:
        for way in range(2):
            for which in range(2):
                fwd_copy(which, d, way).wait_send()
                ret_copy(d, way, which).wait_send()


def body(queries, key_states, value_states, grad_output, block_slot, neighbours):
    H = lax.axis_size("head")
    C = lax.axis_size("ctx")
    rows, width = queries.shape
    chunk = rows // BLOCK_TOK
    per_ctx = chunk * H
    pairs = per_ctx * NBR
    T = per_ctx
    hbm = pl.BlockSpec(memory_space=pltpu.HBM)
    anywhere = pl.BlockSpec(memory_space=pl.ANY)
    out = jax.ShapeDtypeStruct((chunk, BLOCK_TOK, width), jnp.bfloat16)
    dma = pltpu.SemaphoreType.DMA
    low = jnp.bfloat16
    grads = pl.pallas_call(
        functools.partial(main_kernel, H, C),
        out_shape=(out, out, out),
        in_specs=[hbm] * 6,
        out_specs=(anywhere,) * 3,
        scratch_shapes=[
            pltpu.VMEM((1,) + block_slot.shape, jnp.int32), pltpu.VMEM(neighbours.shape[::-1], jnp.int32),
            pltpu.VMEM((3, NBR, 128), jnp.int32), pltpu.SMEM((3, NBR, 128), jnp.int32), dma((4,)),
            pltpu.SemaphoreType.REGULAR((2,)), pltpu.SemaphoreType.REGULAR,
            pltpu.VMEM((T, BLOCK_TOK, 128), low), pltpu.VMEM((T, BLOCK_TOK, 128), low),
            pltpu.VMEM((3 * T, BLOCK_TOK, 128), low), pltpu.VMEM((3 * T, BLOCK_TOK, 128), low),
            pltpu.VMEM((pairs + 1, BLOCK_TOK, 128), jnp.float32),
            pltpu.VMEM((pairs + 1, BLOCK_TOK, 128), jnp.float32),
            pltpu.VMEM((T, BLOCK_TOK, 128), low),
            pltpu.VMEM((2 * T, BLOCK_TOK, 128), low), pltpu.VMEM((2 * T, BLOCK_TOK, 128), low),
            pltpu.VMEM((2 * T, BLOCK_TOK, 128), low), pltpu.VMEM((2 * T, BLOCK_TOK, 128), low),
            pltpu.VMEM((T, BLOCK_TOK, 128), low), pltpu.VMEM((T, BLOCK_TOK, 128), low),
            pltpu.VMEM((chunk, NBR * BLOCK_TOK, 128), jnp.float32), pltpu.VMEM((T, NBR * BLOCK_TOK, 128), jnp.float32),
            pltpu.VMEM((chunk, NBR * BLOCK_TOK, 128), jnp.float32),
            *[pltpu.VMEM((n, 8, 128), jnp.float32) for n in (chunk, T, chunk)],
            dma((4, H)), dma((4, H)), dma((2, H, 2)), dma((2, H, 2)), dma((H,)), dma((H,)),
            dma((2, H, 2)), dma((2, H, 2)), dma((2, H)), dma((2, H)),
        ],
        compiler_params=pltpu.CompilerParams(collective_id=0, has_side_effects=True, vmem_limit_bytes=24 * 2**20),
        name="attention",
    )(*(pltpu.with_memory_space_constraint(x, pltpu.HBM) for x in (block_slot[None], neighbours.T) + tuple(
        x.reshape(chunk, BLOCK_TOK, width) for x in (queries, key_states, value_states, grad_output))))
    grads = pl.pallas_call(
        copy_kernel,
        out_shape=(out, out, out),
        in_specs=[anywhere] * 3,
        out_specs=(anywhere,) * 3,
        scratch_shapes=[dma((3, chunk))],
        compiler_params=pltpu.CompilerParams(vmem_limit_bytes=4 * 2**20),
        name="results",
    )(*grads)
    return tuple(x.reshape(rows, width) for x in grads)


def solution(mesh):
    tokens = P(("band", "ctx", "head"), None)
    in_specs = (tokens, tokens, tokens, tokens, P("band"), P("band", None))
    return jax.shard_map(body, mesh=mesh, in_specs=in_specs, out_specs=(tokens, tokens, tokens), check_vma=False)
```

```python
import functools
import math

import jax
import jax.numpy as jnp
from jax import lax
from jax.experimental import pallas as pl
from jax.experimental.pallas import tpu as pltpu
from jax.sharding import PartitionSpec as P

HEAD_DIM = 64
BLOCK_TOK = 64
NBR = 8
TILE_BLOCKS = 8
MESH = pl.DeviceIdType.MESH
NT = (((1,), (1,)), ((), ()))
NN = (((1,), (0,)), ((), ()))
TN = (((0,), (0,)), ((), ()))


def at_step(step, H):
    return lax.rem(jnp.where(step % 2 == 1, (step + 1) // 2, H - step // 2), H)


def copy_kernel(*refs):
    half = len(refs) // 2
    parts = [(i, k) for i in range(half) for k in range(refs[i].shape[0])]
    copies = [pltpu.make_async_copy(refs[i].at[k], refs[half + i].at[k], refs[-1].at[i, k]) for i, k in parts]
    for copy in copies:
        copy.start()
    for copy in copies:
        copy.wait()


def main_kernel(heads, ctx_size, slot_in, nbr_in, q_in, k_in, v_in, g_in, dq_out, dk_out, dv_out,
                slot_ref, nbr_ref, table_vec, table, table_sem, ring_sem, ctx_sem,
                q_loc, g_loc, k_span, v_span, run_k, run_v, dq_stage, part_k, part_v, back_k, back_v, sum_k, sum_v,
                score_buf, weight_buf, mixed_buf, top_buf, total_buf, stat_buf,
                in_send, in_recv, fwd_send, fwd_recv, dq_send, dq_recv, ret_send, ret_recv, out_send, out_recv):
    H = heads
    h = lax.axis_index("head")
    c = lax.axis_index("ctx")
    per_chunk = q_in.shape[0]
    T = H * per_chunk
    per_ctx = T
    pairs = per_ctx * NBR
    scale = HEAD_DIM ** -0.5
    ctx_prev = lax.rem(c + ctx_size - 1, ctx_size)
    ctx_next = lax.rem(c + 1, ctx_size)
    ctx_peer = (ctx_prev, ctx_next)

    def peer(d):
        return lax.rem(h + d, H)

    def source(d):
        return lax.rem(h + H - d, H)

    def rows(base, chunk):
        return pl.ds(base + chunk * per_chunk, per_chunk)

    def cols(chunk):
        return pl.ds(pl.multiple_of(chunk * 128, 128), 128)

    slot_copy = pltpu.make_async_copy(slot_in, slot_ref, table_sem.at[2])
    nbr_copy = pltpu.make_async_copy(nbr_in, nbr_ref, table_sem.at[3])
    slot_copy.start()
    nbr_copy.start()
    barrier = pltpu.get_barrier_semaphore()
    for d in range(1, H):
        pl.semaphore_signal(barrier, inc=1, device_id={"head": peer(d)}, device_id_type=MESH)
    @pl.when(h == 0)
    def _():
        for p in ctx_peer:
            pl.semaphore_signal(barrier, inc=1, device_id={"ctx": p}, device_id_type=MESH)
        pl.semaphore_wait(barrier, H + 1)

    @pl.when(h != 0)
    def _():
        pl.semaphore_wait(barrier, H - 1)

    order = [0]
    for step in range(1, H):
        order.append(((step + 1) // 2 if step % 2 else H - step // 2) % H)

    incoming = ((k_in, k_span, T), (v_in, v_span, T), (q_in, q_loc, 0), (g_in, g_loc, 0))

    def in_copy(t, d):
        src, dst, base = incoming[t]
        return pltpu.make_async_remote_copy(
            src_ref=src.at[:, :, cols(peer(d))], dst_ref=dst.at[rows(base, h)],
            send_sem=in_send.at[t, d], recv_sem=in_recv.at[t, d],
            device_id={"head": peer(d)}, device_id_type=MESH)

    def in_own(t):
        src, dst, base = incoming[t]
        return pltpu.make_async_copy(src.at[:, :, cols(h)], dst.at[rows(base, h)], in_recv.at[t, 0])

    def in_wait(t, d):
        src, dst, base = incoming[t]
        pltpu.make_async_remote_copy(
            src_ref=src.at[:, :, cols(peer(d))], dst_ref=dst.at[rows(base, source(d))],
            send_sem=in_send.at[t, d], recv_sem=in_recv.at[t, d],
            device_id={"head": peer(d)}, device_id_type=MESH).wait_recv()

    for t in range(4):
        in_own(t).start()
        for d in order[1:]:
            in_copy(t, d).start()

    @pl.when(h == 0)
    def _():
        for way in range(2):
            pl.semaphore_signal(ring_sem.at[way], inc=1, device_id={"ctx": ctx_peer[way]}, device_id_type=MESH)
        for way in range(2):
            pl.semaphore_wait(ring_sem.at[way], 1)
        for d in range(1, H):
            pl.semaphore_signal(ctx_sem, inc=1, device_id={"head": peer(d)}, device_id_type=MESH)

    def crossing_first(start):
        for first in range(2):
            @pl.when(lax.rem(c, 2) == first)
            def _():
                start(first)
                start(1 - first)

    def fwd_copy(t, d, way):
        span = incoming[t][1]
        chunk = source(d)
        return pltpu.make_async_remote_copy(
            src_ref=span.at[rows(T, chunk)],
            dst_ref=span.at[rows(2 * T if way == 0 else 0, chunk)],
            send_sem=fwd_send.at[t, d, way], recv_sem=fwd_recv.at[t, d, way],
            device_id={"ctx": ctx_peer[way]}, device_id_type=MESH)

    slot_copy.wait()
    nbr_copy.wait()
    slots = slot_ref.shape[1]
    slot_row = slot_ref[...]
    nbr = nbr_ref[...]
    slot_lane = lax.broadcasted_iota(jnp.int32, (NBR, slots), 1)
    lane = lax.broadcasted_iota(jnp.int32, (NBR, 128), 1)
    own = lane * NBR + lax.broadcasted_iota(jnp.int32, (NBR, 128), 0)
    targets = jnp.zeros((NBR, 128), jnp.int32)
    for turn in range(per_ctx):
        s = source(order[turn // per_chunk]) * per_chunk + turn % per_chunk
        near = jnp.sum(jnp.where(slot_row == c * per_ctx + s, nbr, 0), axis=1, keepdims=True)
        slot = jnp.sum(jnp.where(slot_lane == near, slot_row, 0), axis=1, keepdims=True)
        target = jnp.zeros_like(slot)
        for region, owner in enumerate((ctx_prev, c, ctx_next)):
            local = slot - owner * per_ctx
            target = jnp.where((local >= 0) & (local < per_ctx), local + region * per_ctx, target)
        targets = jnp.where(lane == turn, target, targets)
    table_vec[0] = targets
    first_half = pltpu.make_async_copy(table_vec.at[pl.ds(0, 1)], table.at[pl.ds(0, 1)], table_sem.at[0])
    first_half.start()
    first_half.wait()

    def chain(turn, carry):
        before, last = carry
        for n in range(NBR):
            target = table[0, n, turn]
            pair = turn * NBR + n
            before = jnp.where((targets == target) & (own > pair), pair, before)
            last = jnp.where(lane == target, pair, last)
        return before, last

    nothing = jnp.full((NBR, 128), pairs, jnp.int32)
    before, last = lax.fori_loop(0, per_ctx, chain, (nothing, nothing))
    table_vec[1] = before
    table_vec[2] = last
    second_half = pltpu.make_async_copy(table_vec.at[pl.ds(1, 2)], table.at[pl.ds(1, 2)], table_sem.at[1])
    second_half.start()
    second_half.wait()

    run_k[pairs] = jnp.zeros(run_k.shape[1:], jnp.float32)
    run_v[pairs] = jnp.zeros(run_v.shape[1:], jnp.float32)

    @pl.when(h != 0)
    def _():
        pl.semaphore_wait(ctx_sem, 1)

    for t in range(2):
        for d in order:
            if d == 0:
                in_own(t).wait()
            else:
                in_wait(t, d)
            crossing_first(lambda way: fwd_copy(t, d, way).start())

    def fwd_wait(t, d, way):
        span = incoming[t][1]
        chunk = source(d)
        pltpu.make_async_remote_copy(
            src_ref=span.at[rows(T, chunk)],
            dst_ref=span.at[rows(2 * T if way == 0 else 0, chunk)],
            send_sem=fwd_send.at[t, d, way], recv_sem=fwd_recv.at[t, d, way],
            device_id={"ctx": ctx_peer[way]}, device_id_type=MESH).wait_recv()

    def span_wait(t):
        for d in order:
            for way in range(2):
                fwd_wait(t, d, way)

    span_wait(0)

    low = (lax.broadcasted_iota(jnp.int32, (1, 128), 1) < HEAD_DIM).astype(jnp.float32)
    low_mask = low.astype(jnp.bfloat16)
    high_mask = (1.0 - low).astype(jnp.bfloat16)
    low_lanes = lax.broadcasted_iota(jnp.int32, (BLOCK_TOK, 128), 1) < HEAD_DIM
    exp_scale = scale * math.log2(math.e)

    tile = TILE_BLOCKS * BLOCK_TOK
    tiles = NBR // TILE_BLOCKS

    def slot_at(turn):
        step = turn // per_chunk
        return source(at_step(step, H)) * per_chunk + turn % per_chunk

    def diagonal(x):
        return jnp.concatenate([x * low_mask, x * high_mask], axis=0)

    def listed(span, turn, r):
        return jnp.concatenate([span[table[0, r * TILE_BLOCKS + n, turn]] for n in range(TILE_BLOCKS)], axis=0)

    def fold(x):
        return x.reshape(tile // 8, 8, 128)

    class Scores:
        def __init__(self, turn, side):
            self.turn, self.side = turn, side
            self.wq = diagonal(q_loc[slot_at(turn)])
            self.top = None

        def tile(self, r):
            part = pl.ds(r * tile, tile)
            scores = lax.dot_general(listed(k_span, self.turn, r), self.wq, NT, preferred_element_type=jnp.float32)
            score_buf[self.side, part, :] = scores
            top = jnp.max(fold(scores), axis=0)
            self.top = top if self.top is None else jnp.maximum(self.top, top)

        def finish(self):
            top_buf[self.side] = self.top

    class Weights:
        def __init__(self, turn, side):
            self.turn, self.side = turn, side
            self.top = jnp.max(top_buf[side], axis=0, keepdims=True)
            self.total = None

        def tile(self, r):
            part = pl.ds(r * tile, tile)
            weights = jnp.exp2((score_buf[self.side, part, :] - self.top) * exp_scale)
            weight_buf[self.turn, part, :] = weights
            total = jnp.sum(fold(weights), axis=0)
            self.total = total if self.total is None else self.total + total

        def finish(self):
            total_buf[self.turn] = self.total

    class Mixed:
        def __init__(self, turn, side):
            self.turn, self.side = turn, side
            self.wg = diagonal(g_loc[slot_at(turn)])
            self.mixed = None

        def tile(self, r):
            part = pl.ds(r * tile, tile)
            grad = lax.dot_general(listed(v_span, self.turn, r), self.wg, NT, preferred_element_type=jnp.float32)
            mixed = weight_buf[self.turn, part, :] * grad
            mixed_buf[self.side, part, :] = mixed
            mixed = jnp.sum(fold(mixed), axis=0)
            self.mixed = mixed if self.mixed is None else self.mixed + mixed

        def finish(self):
            stat_buf[self.side] = self.mixed

    class Gradients:
        def __init__(self, turn, side):
            self.turn, self.side = turn, side
            self.slot = slot_at(turn)
            self.wq, self.wg = diagonal(q_loc[self.slot]), diagonal(g_loc[self.slot])
            self.inverse = 1.0 / jnp.sum(total_buf[turn], axis=0, keepdims=True)
            self.delta = jnp.sum(stat_buf[side], axis=0, keepdims=True) * self.inverse
            self.dq = None

        def tile(self, r):
            part = pl.ds(r * tile, tile)
            prob = weight_buf[self.turn, part, :] * self.inverse
            score_low = (mixed_buf[self.side, part, :] * self.inverse - prob * self.delta).astype(jnp.bfloat16)
            prob_low = prob.astype(jnp.bfloat16)
            dv = lax.dot_general(prob_low, self.wg, NN, preferred_element_type=jnp.float32)
            dk = lax.dot_general(score_low, self.wq, NN, preferred_element_type=jnp.float32)
            dq = lax.dot_general(score_low, listed(k_span, self.turn, r), TN, preferred_element_type=jnp.float32)
            self.dq = dq if self.dq is None else self.dq + dq
            for k in range(TILE_BLOCKS):
                n = r * TILE_BLOCKS + k
                pair = self.turn * NBR + n
                before = table[1, n, self.turn]
                here = slice(k * BLOCK_TOK, (k + 1) * BLOCK_TOK)
                run_k[pair] = dk[here] + run_k[before]
                run_v[pair] = dv[here] + run_v[before]

        def finish(self):
            dq = jnp.where(low_lanes, self.dq[:BLOCK_TOK], self.dq[BLOCK_TOK:]) * scale
            dq_stage[self.slot] = dq.astype(jnp.bfloat16)

    def together(*stages):
        for r in range(tiles):
            for stage in stages:
                stage.tile(r)
        for stage in stages:
            stage.finish()

    def dq_copy(d):
        chunk = source(d)
        return pltpu.make_async_remote_copy(
            src_ref=dq_stage.at[rows(0, chunk)], dst_ref=dq_out.at[:, :, cols(h)],
            send_sem=dq_send.at[d], recv_sem=dq_recv.at[d],
            device_id={"head": chunk}, device_id_type=MESH)

    def dq_own():
        return pltpu.make_async_copy(dq_stage.at[rows(0, h)], dq_out.at[:, :, cols(h)], dq_recv.at[0])

    turns = H * per_chunk
    in_own(2).wait()
    together(*[Scores(k, k) for k in range(per_chunk)])

    def first_step(step, carry):
        in_wait(2, at_step(step, H))
        turn = step * per_chunk
        together(*[Weights(turn - per_chunk + k, k) for k in range(per_chunk)],
                 *[Scores(turn + k, k) for k in range(per_chunk)])
        return carry

    lax.fori_loop(1, H, first_step, 0)
    together(*[Weights(turns - per_chunk + k, k) for k in range(per_chunk)])

    span_wait(1)
    in_own(3).wait()
    together(*[Mixed(k, k) for k in range(per_chunk)])

    def second_step(step, carry):
        in_wait(3, at_step(step, H))

        @pl.when(step == 2)
        def _():
            dq_own().start()

        @pl.when(step > 2)
        def _():
            dq_copy(at_step(step - 2, H)).start()

        turn = step * per_chunk
        together(*[Gradients(turn - per_chunk + k, k) for k in range(per_chunk)],
                 *[Mixed(turn + k, k) for k in range(per_chunk)])
        return carry

    lax.fori_loop(1, H, second_step, 0)
    if H == 2:
        dq_own().start()
    else:
        dq_copy(order[H - 2]).start()
    together(*[Gradients(turns - per_chunk + k, k) for k in range(per_chunk)])
    dq_copy(order[H - 1]).start()

    back_order = order[::-1]

    def ret_copy(d, way, which):
        chunk = peer(d)
        part = (part_k, part_v)[which]
        back = (back_k, back_v)[which]
        return pltpu.make_async_remote_copy(
            src_ref=part.at[rows(way * T, chunk)], dst_ref=back.at[rows(way * T, chunk)],
            send_sem=ret_send.at[which, d, way], recv_sem=ret_recv.at[which, d, way],
            device_id={"ctx": ctx_peer[way]}, device_id_type=MESH)

    for d in back_order:
        chunk = peer(d)
        for way in range(2):
            region = 0 if way == 0 else 2
            for k in range(per_chunk):
                block = chunk * per_chunk + k
                end = table[2, 0, region * per_ctx + block]
                part_k[way * T + block] = (run_k[end] * scale).astype(jnp.bfloat16)
                part_v[way * T + block] = run_v[end].astype(jnp.bfloat16)
        crossing_first(lambda way: [ret_copy(d, way, which).start() for which in range(2)])

    def out_copy(d, which):
        chunk = peer(d)
        return pltpu.make_async_remote_copy(
            src_ref=(sum_k, sum_v)[which].at[rows(0, chunk)], dst_ref=(dk_out, dv_out)[which].at[:, :, cols(h)],
            send_sem=out_send.at[which, d], recv_sem=out_recv.at[which, d],
            device_id={"head": chunk}, device_id_type=MESH)

    def out_own(which):
        return pltpu.make_async_copy(
            (sum_k, sum_v)[which].at[rows(0, h)], (dk_out, dv_out)[which].at[:, :, cols(h)], out_recv.at[which, 0])

    for d in back_order:
        chunk = peer(d)
        for way in range(2):
            for which in range(2):
                ret_copy(d, way, which).wait_recv()
        for k in range(per_chunk):
            block = chunk * per_chunk + k
            end = table[2, 0, per_ctx + block]
            sum_k[block] = (run_k[end] * scale + back_k[block].astype(jnp.float32)
                            + back_k[T + block].astype(jnp.float32)).astype(jnp.bfloat16)
            sum_v[block] = (run_v[end] + back_v[block].astype(jnp.float32)
                            + back_v[T + block].astype(jnp.float32)).astype(jnp.bfloat16)
        for which in range(2):
            if d == 0:
                out_own(which).start()
            else:
                out_copy(d, which).start()

    dq_own().wait()
    for which in range(2):
        out_own(which).wait()
    for d in order[1:]:
        for t in range(4):
            in_copy(t, d).wait_send()
        dq_copy(d).wait_send()
        pltpu.make_async_remote_copy(
            src_ref=dq_stage.at[rows(0, peer(d))], dst_ref=dq_out.at[:, :, cols(peer(d))],
            send_sem=dq_send.at[d], recv_sem=dq_recv.at[d],
            device_id={"head": peer(d)}, device_id_type=MESH).wait_recv()
        for which in range(2):
            out_copy(d, which).wait_send()
            pltpu.make_async_remote_copy(
                src_ref=(sum_k, sum_v)[which].at[rows(0, source(d))],
                dst_ref=(dk_out, dv_out)[which].at[:, :, cols(source(d))],
                send_sem=out_send.at[which, d], recv_sem=out_recv.at[which, d],
                device_id={"head": source(d)}, device_id_type=MESH).wait_recv()
    for d in order:
        for way in range(2):
            for which in range(2):
                fwd_copy(which, d, way).wait_send()
                ret_copy(d, way, which).wait_send()


def body(queries, key_states, value_states, grad_output, block_slot, neighbours):
    H = lax.axis_size("head")
    C = lax.axis_size("ctx")
    rows, width = queries.shape
    chunk = rows // BLOCK_TOK
    per_ctx = chunk * H
    pairs = per_ctx * NBR
    T = per_ctx
    hbm = pl.BlockSpec(memory_space=pltpu.HBM)
    anywhere = pl.BlockSpec(memory_space=pl.ANY)
    out = jax.ShapeDtypeStruct((chunk, BLOCK_TOK, width), jnp.bfloat16)
    dma = pltpu.SemaphoreType.DMA
    low = jnp.bfloat16
    grads = pl.pallas_call(
        functools.partial(main_kernel, H, C),
        out_shape=(out, out, out),
        in_specs=[hbm] * 6,
        out_specs=(anywhere,) * 3,
        scratch_shapes=[
            pltpu.VMEM((1,) + block_slot.shape, jnp.int32), pltpu.VMEM(neighbours.shape[::-1], jnp.int32),
            pltpu.VMEM((3, NBR, 128), jnp.int32), pltpu.SMEM((3, NBR, 128), jnp.int32), dma((4,)),
            pltpu.SemaphoreType.REGULAR((2,)), pltpu.SemaphoreType.REGULAR,
            pltpu.VMEM((T, BLOCK_TOK, 128), low), pltpu.VMEM((T, BLOCK_TOK, 128), low),
            pltpu.VMEM((3 * T, BLOCK_TOK, 128), low), pltpu.VMEM((3 * T, BLOCK_TOK, 128), low),
            pltpu.VMEM((pairs + 1, BLOCK_TOK, 128), jnp.float32),
            pltpu.VMEM((pairs + 1, BLOCK_TOK, 128), jnp.float32),
            pltpu.VMEM((T, BLOCK_TOK, 128), low),
            pltpu.VMEM((2 * T, BLOCK_TOK, 128), low), pltpu.VMEM((2 * T, BLOCK_TOK, 128), low),
            pltpu.VMEM((2 * T, BLOCK_TOK, 128), low), pltpu.VMEM((2 * T, BLOCK_TOK, 128), low),
            pltpu.VMEM((T, BLOCK_TOK, 128), low), pltpu.VMEM((T, BLOCK_TOK, 128), low),
            pltpu.VMEM((chunk, NBR * BLOCK_TOK, 128), jnp.float32), pltpu.VMEM((T, NBR * BLOCK_TOK, 128), jnp.float32),
            pltpu.VMEM((chunk, NBR * BLOCK_TOK, 128), jnp.float32),
            *[pltpu.VMEM((n, 8, 128), jnp.float32) for n in (chunk, T, chunk)],
            dma((4, H)), dma((4, H)), dma((2, H, 2)), dma((2, H, 2)), dma((H,)), dma((H,)),
            dma((2, H, 2)), dma((2, H, 2)), dma((2, H)), dma((2, H)),
        ],
        compiler_params=pltpu.CompilerParams(collective_id=0, has_side_effects=True, vmem_limit_bytes=24 * 2**20),
        name="attention",
    )(*(pltpu.with_memory_space_constraint(x, pltpu.HBM) for x in (block_slot[None], neighbours.T) + tuple(
        x.reshape(chunk, BLOCK_TOK, width) for x in (queries, key_states, value_states, grad_output))))
    grads = pl.pallas_call(
        copy_kernel,
        out_shape=(out, out, out),
        in_specs=[anywhere] * 3,
        out_specs=(anywhere,) * 3,
        scratch_shapes=[dma((3, chunk))],
        compiler_params=pltpu.CompilerParams(vmem_limit_bytes=4 * 2**20),
        name="results",
    )(*grads)
    return tuple(x.reshape(rows, width) for x in grads)


def solution(mesh):
    tokens = P(("band", "ctx", "head"), None)
    in_specs = (tokens, tokens, tokens, tokens, P("band"), P("band", None))
    return jax.shard_map(body, mesh=mesh, in_specs=in_specs, out_specs=(tokens, tokens, tokens), check_vma=False)
```
